128 devices in a mesh: vocab: 128 (over x, z, y, core).
Axes of the slice: x: 4, y: 4, z: 4, core: 2. Of those that a mesh axis runs over, the one named last changes fastest.
Arguments:
- hidden_states: bfloat16 [512, 5120], P('vocab'), may hold values from -8 to 8
- head_weight: bfloat16 [5120, 131072], P(None, 'vocab'), may hold values from -0.25 to 0.25
- teacher_logits: bfloat16 [4, 256, 128, 128], P(None, None, 'vocab'), may hold values from -15 to 260
- block_lists: int32 [4, 256], replicated, may hold values from 0 to 1023, as said below
- row_reader: int32 [4, 128], replicated, may hold values from 0 to 127, each once within a row
- tail_mass: float32 [512], replicated, may hold values from 0.05 to 0.5
- token_weight: float32 [512], replicated, may hold values from 1 to 8
Outputs:
- token_loss: float32 [512], P('vocab')
- grad_head: bfloat16 [5120, 131072], P(None, 'vocab')
- grad_hidden: bfloat16 [512, 5120], P('vocab')
The draws below stay inside these ranges and needn't reach their ends.
Inputs may be any that keep to these rules, and one draw needn't show every extreme that they name: `block_lists`: for each token block the 256 listed vocabulary blocks are distinct; at most 4 of them lie in any slab of 8 consecutive blocks starting at a multiple of 8, and in every token block some slab holds exactly 4. `row_reader`: each row is a permutation.
All inputs are finite; a program needn't handle non-finite values.
Results may differ from the reference program's by a relative error of at most 0.0048.
Values may be sent and summed in bfloat16 or wider, within the bound.
A program may use at most 128 MiB of HBM per device.

```python
import math
import jax
import jax.numpy as jnp
from jax import lax

D = 5120
BLK = 128
VB_DEV = 8
VOCAB = 131072
NVB = 1024
TOKEN_BLOCKS = 4
TOKENS = 512
K = 256
MOST = 4


def head_matrix(key):
    values = jax.random.normal(jax.random.fold_in(key, 101), (D, VOCAB), jnp.float32)
    return jnp.clip(values * 0.042, -0.25, 0.25)


def draw_head_weight(key, part):
    return head_matrix(key).astype(jnp.bfloat16)


def draw_hidden_states(key, part):
    values = jax.random.normal(jax.random.fold_in(key, 5), (TOKENS, D), jnp.float32)
    return jnp.clip(values, -6.0, 6.0).astype(jnp.bfloat16)


def draw_teacher_logits(key, part):
    shape = (TOKEN_BLOCKS, K, BLK, BLK)
    values = jax.random.normal(jax.random.fold_in(key, 21), shape, jnp.float32) * 3.0
    return jnp.clip(values, -15.0, 15.0).astype(jnp.bfloat16)


def draw_block_lists(key, part):
    owners = NVB // VB_DEV
    slot_positions = owners * MOST
    single_step = 262144
    preference_boost = jax.random.randint(jax.random.fold_in(key, 31), (owners,), 0, 3)
    random_jitter = jax.random.randint(jax.random.fold_in(key, 33), (TOKEN_BLOCKS, owners, MOST), 0, 2 * single_step)
    required_pick = jax.random.randint(jax.random.fold_in(key, 35), (TOKEN_BLOCKS, 1, 1), 0, owners)
    owner_sequence = jnp.arange(owners, dtype=jnp.int32)[None, :, None]
    extra_reward = jnp.where(owner_sequence == required_pick, 5 * single_step, preference_boost[None, :, None] * single_step)
    ranking_value = (extra_reward + random_jitter).reshape(TOKEN_BLOCKS, slot_positions) * slot_positions + jnp.arange(slot_positions, dtype=jnp.int32)[None, :]
    chosen = lax.top_k(ranking_value, K)[1].astype(jnp.int32)
    owner_pick = chosen // MOST
    slot_pick = chosen % MOST
    order_keys = jax.random.randint(jax.random.fold_in(key, 37), (TOKEN_BLOCKS, owners, VB_DEV), 0, 1048576) * VB_DEV + jnp.arange(VB_DEV, dtype=jnp.int32)[None, None, :]
    local_order = jnp.argsort(order_keys, axis=2).astype(jnp.int32)
    placed = jax.vmap(lambda table, owner_row, slot_row: table[owner_row, slot_row])(local_order, owner_pick, slot_pick)
    return (owner_pick * VB_DEV + placed).astype(jnp.int32)


def setup_inputs(seed: int = 0) -> dict:
    arg_keys = jax.random.split(jax.random.key(seed), 8)
    hidden_states = draw_hidden_states(jax.random.fold_in(arg_keys[7], 71), 0)
    head_weight = draw_head_weight(jax.random.fold_in(arg_keys[7], 71), 0)
    teacher_logits = draw_teacher_logits(jax.random.fold_in(arg_keys[7], 71), 0)
    block_lists = draw_block_lists(jax.random.fold_in(arg_keys[7], 71), 0)
    row_reader = jax.vmap(lambda own: jax.random.permutation(own, BLK))(jax.random.split(arg_keys[4], TOKEN_BLOCKS)).reshape((TOKEN_BLOCKS, BLK)).astype(jnp.int32)
    tail_mass = jnp.clip(jax.random.uniform(arg_keys[5], (TOKENS,), jnp.float32, 0.05, 0.5), 0.05, 0.5)
    token_weight = jnp.clip(jnp.exp(jax.random.uniform(arg_keys[6], (TOKENS,), jnp.float32, math.log(1.0), math.log(8.0))), 1.0, 8.0)
    return dict(hidden_states=hidden_states, head_weight=head_weight, teacher_logits=teacher_logits, block_lists=block_lists, row_reader=row_reader, tail_mass=tail_mass, token_weight=token_weight)


def reference(hidden_states, head_weight, teacher_logits, block_lists, row_reader, tail_mass, token_weight):
    logits = jnp.dot(hidden_states, head_weight, preferred_element_type=jnp.float32)
    vocab_blocks = VOCAB // BLK
    inverse = jnp.argsort(row_reader, axis=1).astype(jnp.int32)
    token_rows = jax.vmap(lambda stored, order: stored[:, order, :])(teacher_logits, inverse)
    block_rows = jnp.arange(TOKEN_BLOCKS, dtype=jnp.int32)[:, None]
    teacher_dense = jnp.zeros((TOKEN_BLOCKS, vocab_blocks, BLK, BLK), jnp.float32)
    teacher_dense = teacher_dense.at[block_rows, block_lists].set(token_rows.astype(jnp.float32))
    listed = jnp.zeros((TOKEN_BLOCKS, vocab_blocks), jnp.float32).at[block_rows, block_lists].set(1.0)
    teacher_values = teacher_dense.transpose(0, 2, 1, 3).reshape(TOKEN_BLOCKS, BLK, VOCAB)
    listed_mask = (jnp.repeat(listed, BLK, axis=1) > 0.5)[:, None, :]
    scores = logits.reshape(TOKEN_BLOCKS, BLK, VOCAB)
    student_max = jnp.max(scores, axis=-1, keepdims=True)
    log_norm = student_max + jnp.log(jnp.sum(jnp.exp(scores - student_max), axis=-1, keepdims=True))
    teacher_max = jnp.max(jnp.where(listed_mask, teacher_values, -jnp.inf), axis=-1, keepdims=True)
    teacher_sum = jnp.sum(jnp.where(listed_mask, jnp.exp(teacher_values - teacher_max), 0.0), axis=-1, keepdims=True)
    tail_share = tail_mass.reshape(TOKEN_BLOCKS, BLK, 1)
    unlisted = VOCAB - BLK * K
    log_teacher = jnp.where(listed_mask, jnp.log(1.0 - tail_share) + teacher_values - teacher_max - jnp.log(teacher_sum), jnp.log(tail_share / unlisted))
    teacher_prob = jnp.exp(log_teacher)
    token_loss = jnp.sum(teacher_prob * (log_teacher - scores + log_norm), axis=-1).reshape(TOKENS)
    student_prob = jnp.exp(scores - log_norm)
    weight = token_weight.reshape(TOKEN_BLOCKS, BLK, 1)
    grad_logits = (weight * (student_prob - teacher_prob)).astype(jnp.bfloat16).reshape(TOKENS, VOCAB)
    grad_head = lax.dot_general(hidden_states, grad_logits, (((0,), (0,)), ((), ())), preferred_element_type=jnp.float32).astype(jnp.bfloat16)
    grad_hidden = lax.dot_general(grad_logits, head_weight, (((1,), (1,)), ((), ())), preferred_element_type=jnp.float32).astype(jnp.bfloat16)
    return token_loss, grad_head, grad_hidden
```

```python
import functools

import jax
import jax.numpy as jnp
from jax import lax
from jax.experimental import pallas as pl
from jax.experimental.pallas import tpu as pltpu
from jax.sharding import Mesh
from jax.sharding import PartitionSpec as P

MOST = 4
AXES = ("x", "z", "y", "c")
N = 4
D = 5120
CHUNKS = ((0, 1280, "x", "z"), (1280, 1280, "z", "x"), (2560, 1280, "x", "z"), (3840, 1280, "z", "x"))
NC = len(CHUNKS)
DMA = pltpu.SemaphoreType.DMA
REGULAR = pltpu.SemaphoreType.REGULAR
VM = pl.BlockSpec(memory_space=pltpu.VMEM)
ANY = pl.BlockSpec(memory_space=pl.ANY)


def spot():
    return {a: lax.axis_index(a) for a in AXES}


def moved(pos, axis, step):
    if axis == "c":
        return {"c": 1 - pos["c"]}
    return {axis: lax.rem(pos[axis] + step + N, N)}


def remote(src, dst, send, recv, device):
    return pltpu.make_async_remote_copy(
        src_ref=src, dst_ref=dst, send_sem=send, recv_sem=recv,
        device_id=device, device_id_type=pl.DeviceIdType.MESH,
    )


def greet(pos, partners):
    barrier = pltpu.get_barrier_semaphore()
    for device in partners:
        pl.semaphore_signal(barrier, inc=1, device_id=device, device_id_type=pl.DeviceIdType.MESH)
    pl.semaphore_wait(barrier, len(partners))


def lines(pos, axes):
    return [moved(pos, a, s) for a in axes for s in ((1,) if a == "c" else (1, 2, 3))]


def gather_chunk(pos, f, full, asend, arecv, bsend, brecv, csend, crecv):
    start, width, A, B = CHUNKS[f]
    half = width // 2
    a, b, c = pos[A], pos[B], pos["c"]
    every, low, high = pl.ds(start, width), pl.ds(start, half), pl.ds(start + half, half)
    sent = []

    def unit(off_a, off_b, cols):
        at = {A: lax.rem(a + off_a + N, N), B: lax.rem(b + off_b + N, N)}
        return full.at[at["x"], at["z"], c, :, cols]

    def send(ref, send_sem, recv_sem, axis, step):
        copy = remote(ref, ref, send_sem, recv_sem, moved(pos, axis, step))
        copy.start()
        sent.append(copy)

    def arrived(ref, recv_sem):
        remote(ref, ref, recv_sem, recv_sem, moved(pos, "c", 1)).wait_recv()

    offs = (0, -1, 1, 2)

    def onward(j):
        ref = unit(offs[j], 0, every)
        send(ref, bsend.at[f, j, 0], brecv.at[f, j, 0], B, 1)
        send(ref, bsend.at[f, j, 1], brecv.at[f, j, 1], B, -1)
        across(j, 0)

    def across(j, k):
        send(unit(offs[j], offs[k], every), csend.at[f, j, k], crecv.at[f, j, k], "c", 1)

    ref = unit(0, 0, every)
    send(ref, asend.at[f, 0], arecv.at[f, 0], A, 1)
    send(ref, asend.at[f, 1], arecv.at[f, 1], A, -1)
    onward(0)
    yield
    arrived(unit(-1, 0, every), arecv.at[f, 0])
    send(unit(-1, 0, low), asend.at[f, 2], arecv.at[f, 2], A, 1)
    onward(1)
    arrived(unit(1, 0, every), arecv.at[f, 1])
    send(unit(1, 0, high), asend.at[f, 3], arecv.at[f, 3], A, -1)
    onward(2)
    yield

    def relay(j):
        arrived(unit(offs[j], -1, every), brecv.at[f, j, 0])
        send(unit(offs[j], -1, low), bsend.at[f, j, 2], brecv.at[f, j, 2], B, 1)
        across(j, 1)
        arrived(unit(offs[j], 1, every), brecv.at[f, j, 1])
        send(unit(offs[j], 1, high), bsend.at[f, j, 3], brecv.at[f, j, 3], B, -1)
        across(j, 2)

    relay(0)
    yield
    arrived(unit(2, 0, low), arecv.at[f, 2])
    arrived(unit(2, 0, high), arecv.at[f, 3])
    onward(3)
    yield
    relay(1)
    relay(2)
    yield
    relay(3)
    yield
    for j in range(4):
        arrived(unit(offs[j], 2, low), brecv.at[f, j, 2])
        arrived(unit(offs[j], 2, high), brecv.at[f, j, 3])
        across(j, 3)
    yield
    for j in range(4):
        for k in range(4):
            at = {A: lax.rem(a + offs[j] + N, N), B: lax.rem(b + offs[k] + N, N)}
            arrived(full.at[at["x"], at["z"], 1 - c, :, every], crecv.at[f, j, k])
    for copy in sent:
        copy.wait_send()


def run_all(gens):
    gens = list(gens)
    while gens:
        for g in list(gens):
            try:
                next(g)
            except StopIteration:
                gens.remove(g)


def gather_kernel(h_ref, out_ref, full, inc, rows, wide, ysend, yrecv, asend, arecv, bsend, brecv,
                  csend, crecv, tsend, trecv, own, gz, gx, gc):
    pos = spot()
    x, z, y, c = (pos[a] for a in AXES)
    me = ((x * N + z) * N + y) * 2 + c
    greet(pos, lines(pos, AXES))

    def everyone(sem, axes):
        partners = lines(pos, axes)
        for device in partners:
            pl.semaphore_signal(sem, inc=1, device_id=device, device_id_type=pl.DeviceIdType.MESH)
        pl.semaphore_wait(sem, len(partners))

    first = []
    for d in (1, 2, 3):
        copy = remote(h_ref, rows.at[y], ysend.at[d - 1], yrecv.at[d - 1], moved(pos, "y", d))
        copy.start()
        first.append(copy)
    mine = pltpu.make_async_copy(h_ref, rows.at[y], own.at[0])
    mine.start()
    keep = pltpu.make_async_copy(out_ref.at[me], inc.at[me], own.at[1])
    keep.start()
    everyone(gz, ("z",))
    mine.wait()
    for d in (1, 2, 3):
        ref = rows.at[lax.rem(y - d + N, N)]
        remote(ref, ref, ysend.at[d - 1], yrecv.at[d - 1], moved(pos, "y", d)).wait_recv()
    for k in range(N):
        wide[4 * k : 4 * k + 4, :] = rows[k].astype(jnp.float32)
    full[x, z, c] = wide[...].astype(jnp.bfloat16)
    gens = [gather_chunk(pos, f, full, asend, arecv, bsend, brecv, csend, crecv) for f in range(NC)]
    for g in gens:
        next(g)
    everyone(gx, ("x",))
    everyone(gc, ("c",))

    def one(k, carry):
        to = lax.rem(me + k, 128)
        device = {"x": to // 32, "z": lax.rem(to // 8, N), "y": lax.rem(to // 2, N), "c": lax.rem(to, 2)}
        remote(out_ref.at[to], inc.at[me], tsend, trecv, device).start()
        return carry

    lax.fori_loop(1, 128, one, 0)
    run_all(gens)
    for copy in first:
        copy.wait_send()
    part = inc.at[pl.ds(0, 127)]
    remote(part, part, tsend, trecv, moved(pos, "c", 1)).wait()
    keep.wait()


def gather(hidden, outgoing):
    return pl.pallas_call(
        gather_kernel,
        out_shape=(
            jax.ShapeDtypeStruct((N, N, 2, 16, D), jnp.bfloat16),
            jax.ShapeDtypeStruct(outgoing.shape, jnp.bfloat16),
        ),
        in_specs=[VM, VM],
        out_specs=(VM, VM),
        scratch_shapes=[
            pltpu.VMEM((N, 4, D), jnp.bfloat16),
            pltpu.VMEM((16, D), jnp.float32),
            DMA((3,)), DMA((3,)),
            DMA((NC, 4)), DMA((NC, 4)),
            DMA((NC, 4, 4)), DMA((NC, 4, 4)),
            DMA((NC, 4, 4)), DMA((NC, 4, 4)),
            DMA, DMA, DMA((2,)),
            REGULAR, REGULAR, REGULAR,
        ],
        compiler_params=pltpu.CompilerParams(collective_id=0, has_side_effects=True, vmem_limit_bytes=60 << 20),
        name="gather",
    )(hidden, outgoing)


def merge(parts):
    top = parts[0][0]
    for p in parts[1:]:
        top = jnp.maximum(top, p[0])
    row = lax.broadcasted_iota(jnp.int32, (8, 128), 0)
    sums = [0.0, 0.0, 0.0]
    for p in parts:
        scale = jnp.exp(p[0] - top)
        sums[0] += p[1] * scale
        sums[1] += p[2] * jnp.where(row < 4, 1.0, scale)
        sums[2] += p[3] * scale
    return [top] + sums


def stats_kernel(st, out, near, mid, far, send1, recv1, send2, recv2):
    pos = spot()
    x, z, y, c = (pos[a] for a in AXES)
    plane = [{"z": lax.rem(z + dz, N), "y": lax.rem(y + dy, N)} for dz in range(N) for dy in range(N) if dz or dy]
    line = [{"x": lax.rem(x + dx, N), "c": lax.rem(c + dc, 2)} for dx in range(N) for dc in range(2) if dx or dc]
    greet(pos, plane + line)
    for device in plane:
        remote(st, near.at[z * N + y], send1, recv1, device).start()
    near[z * N + y] = st[...]
    group = near.at[pl.ds(0, 15)]
    remote(group, group, send1, recv1, plane[0]).wait()
    for k, v in enumerate(merge([near[i] for i in range(16)])):
        mid[k] = v
    for device in line:
        remote(mid, far.at[x * 2 + c], send2, recv2, device).start()
    far[x * 2 + c] = mid[...]
    group = far.at[pl.ds(0, 7)]
    remote(group, group, send2, recv2, line[0]).wait()
    for k, v in enumerate(merge([far[i] for i in range(8)])):
        out[k] = v


def stats_merge(st):
    return pl.pallas_call(
        stats_kernel,
        out_shape=jax.ShapeDtypeStruct(st.shape, st.dtype),
        in_specs=[VM],
        out_specs=VM,
        scratch_shapes=[
            pltpu.VMEM((16,) + st.shape, st.dtype),
            pltpu.VMEM(st.shape, st.dtype),
            pltpu.VMEM((8,) + st.shape, st.dtype),
            DMA, DMA, DMA, DMA,
        ],
        compiler_params=pltpu.CompilerParams(collective_id=1, has_side_effects=True),
        name="stats_merge",
    )(st)


W = CHUNKS[0][1]
TILE = 256


def scatter_chunk(pos, f, gl, w, part, cs, cr, bs1, br1, bs2, br2, red, as1, ar1, as2, ar2, ys, yr,
                  out, csem, bsem, asem, ysem):
    start, width, A, B = CHUNKS[f]
    half = width // 2
    a, b, c, y = pos[A], pos[B], pos["c"], pos["y"]
    f32, bf16 = jnp.float32, jnp.bfloat16
    sent = []

    def index(ia, ib):
        at = {A: ia, B: ib}
        return at["x"] * N + at["z"]

    def shift(p, s):
        return lax.rem(p + s + N, N)

    def send(src, dst, sems, k, axis, step):
        copy = remote(src, dst, sems.at[0, f, k], sems.at[1, f, k], moved(pos, axis, step))
        copy.start()
        sent.append(copy)

    def arrived(ref, sems, k):
        remote(ref, ref, sems.at[0, f, k], sems.at[1, f, k], moved(pos, "c", 1)).wait_recv()

    def product(i, carry):
        rows = w[pl.ds(pl.multiple_of(start + i * TILE, TILE), TILE), :]
        got = lax.dot_general(gl[...], rows, (((1,), (1,)), ((), ())), preferred_element_type=f32)
        part[f, :, :, :, pl.ds(pl.multiple_of(i * TILE, TILE), TILE)] = got.reshape(16, 2, 16, TILE)
        return carry

    lax.fori_loop(0, width // TILE, product, 0)

    def other(u, carry):
        cs[f, u] = part[f, u, 1 - c].astype(bf16)
        return carry

    lax.fori_loop(0, 16, other, 0)
    send(cs.at[f], cr.at[f], csem, 0, "c", 1)
    yield
    arrived(cr.at[f], csem, 0)

    def chip(u):
        return part[f, u, c] + cr[f, u].astype(f32)

    def opposite(i, carry):
        v = chip(index(i, shift(b, 2))).astype(bf16)
        bs1[f, 0, i] = v[:, :half]
        bs1[f, 1, i] = v[:, half:]
        return carry

    lax.fori_loop(0, N, opposite, 0)
    send(bs1.at[f, 0], br1.at[f, 0], bsem, 0, B, 1)
    send(bs1.at[f, 1], br1.at[f, 1], bsem, 1, B, -1)
    yield
    arrived(br1.at[f, 0], bsem, 0)

    def up(i, carry):
        v = chip(index(i, shift(b, 1)))
        bs2[f, 0, i, :, :half] = (v[:, :half] + br1[f, 0, i].astype(f32)).astype(bf16)
        bs2[f, 0, i, :, half:] = v[:, half:].astype(bf16)
        return carry

    lax.fori_loop(0, N, up, 0)
    send(bs2.at[f, 0], br2.at[f, 0], bsem, 2, B, 1)
    arrived(br1.at[f, 1], bsem, 1)

    def down(i, carry):
        v = chip(index(i, shift(b, -1)))
        bs2[f, 1, i, :, :half] = v[:, :half].astype(bf16)
        bs2[f, 1, i, :, half:] = (v[:, half:] + br1[f, 1, i].astype(f32)).astype(bf16)
        return carry

    lax.fori_loop(0, N, down, 0)
    send(bs2.at[f, 1], br2.at[f, 1], bsem, 3, B, -1)
    yield
    arrived(br2.at[f, 0], bsem, 2)
    arrived(br2.at[f, 1], bsem, 3)

    def kept(i, carry):
        red[f, i] = chip(index(i, b)) + br2[f, 0, i].astype(f32) + br2[f, 1, i].astype(f32)
        return carry

    lax.fori_loop(0, N, kept, 0)
    v = red[f, shift(a, 2)].astype(bf16)
    as1[f, 0] = v[:, :half]
    as1[f, 1] = v[:, half:]
    send(as1.at[f, 0], ar1.at[f, 0], asem, 0, A, 1)
    send(as1.at[f, 1], ar1.at[f, 1], asem, 1, A, -1)
    yield
    arrived(ar1.at[f, 0], asem, 0)
    v = red[f, shift(a, 1)]
    as2[f, 0, :, :half] = (v[:, :half] + ar1[f, 0].astype(f32)).astype(bf16)
    as2[f, 0, :, half:] = v[:, half:].astype(bf16)
    send(as2.at[f, 0], ar2.at[f, 0], asem, 2, A, 1)
    arrived(ar1.at[f, 1], asem, 1)
    v = red[f, shift(a, -1)]
    as2[f, 1, :, :half] = v[:, :half].astype(bf16)
    as2[f, 1, :, half:] = (v[:, half:] + ar1[f, 1].astype(f32)).astype(bf16)
    send(as2.at[f, 1], ar2.at[f, 1], asem, 3, A, -1)
    yield
    arrived(ar2.at[f, 0], asem, 2)
    arrived(ar2.at[f, 1], asem, 3)
    v = red[f, a] + ar2[f, 0].astype(f32) + ar2[f, 1].astype(f32)
    for k in range(N):
        ys[f, k] = v[4 * k : 4 * k + 4, :]
    for d in (1, 2, 3):
        send(ys.at[f, shift(y, d)], yr.at[f, d - 1], ysem, d - 1, "y", d)
    yield
    for d in (1, 2, 3):
        arrived(yr.at[f, d - 1], ysem, d - 1)
    total = ys[f, y] + yr[f, 0] + yr[f, 1] + yr[f, 2]
    out[:, start : start + width] = total.astype(bf16)
    for copy in sent:
        copy.wait_send()


def scatter_kernel(gl, w_hbm, out, w, part, cs, cr, bs1, br1, bs2, br2, red, as1, ar1, as2, ar2, ys, yr,
                   csem, bsem, asem, ysem, wsem):
    pos = spot()
    loads = []
    for f, (start, width, _, _) in enumerate(CHUNKS):
        copy = pltpu.make_async_copy(w_hbm.at[pl.ds(start, width)], w.at[pl.ds(start, width)], wsem.at[f])
        copy.start()
        loads.append(copy)
    greet(pos, lines(pos, AXES))
    live = []
    for f in range(NC):
        loads[f].wait()
        g = scatter_chunk(pos, f, gl, w, part, cs, cr, bs1, br1, bs2, br2, red, as1, ar1, as2, ar2, ys, yr,
                          out, csem, bsem, asem, ysem)
        next(g)
        for other in live:
            next(other)
        live.append(g)
    run_all(live)


def scatter(gl, head):
    bf16, f32 = jnp.bfloat16, jnp.float32
    half = W // 2
    return pl.pallas_call(
        scatter_kernel,
        out_shape=jax.ShapeDtypeStruct((4, D), bf16),
        in_specs=[VM, ANY],
        out_specs=VM,
        scratch_shapes=[
            pltpu.VMEM(head.shape, bf16),
            pltpu.VMEM((NC, 16, 2, 16, W), f32),
            pltpu.VMEM((NC, 16, 16, W), bf16), pltpu.VMEM((NC, 16, 16, W), bf16),
            pltpu.VMEM((NC, 2, N, 16, half), bf16), pltpu.VMEM((NC, 2, N, 16, half), bf16),
            pltpu.VMEM((NC, 2, N, 16, W), bf16), pltpu.VMEM((NC, 2, N, 16, W), bf16),
            pltpu.VMEM((NC, N, 16, W), f32),
            pltpu.VMEM((NC, 2, 16, half), bf16), pltpu.VMEM((NC, 2, 16, half), bf16),
            pltpu.VMEM((NC, 2, 16, W), bf16), pltpu.VMEM((NC, 2, 16, W), bf16),
            pltpu.VMEM((NC, N, 4, W), f32), pltpu.VMEM((NC, 3, 4, W), f32),
            DMA((2, NC, 1)), DMA((2, NC, 4)), DMA((2, NC, 4)), DMA((2, NC, 3)), DMA((NC,)),
        ],
        compiler_params=pltpu.CompilerParams(collective_id=2, has_side_effects=True, vmem_limit_bytes=60 << 20),
        name="scatter",
    )(gl, head)


def on_device(
    hidden_states, head_weight, teacher_logits, block_lists, row_reader, tail_mass, token_weight
):
    blocks, listed_count, stored_rows, block_side = teacher_logits.shape
    slab_width = head_weight.shape[1]
    slab_blocks = slab_width // block_side
    devices = 128
    x, z, y, c = (lax.axis_index(a) for a in AXES)
    rank_self = ((x * N + z) * N + y) * 2 + c
    tokens = blocks * block_side
    owner_dev = block_lists // slab_blocks
    earlier = lax.broadcasted_iota(
        jnp.int32, (1, listed_count, listed_count), 2
    ) < lax.broadcasted_iota(jnp.int32, (1, listed_count, listed_count), 1)
    same_owner = owner_dev[:, :, None] == owner_dev[:, None, :]
    order_rank = jnp.sum((same_owner & earlier).astype(jnp.int32), axis=2)
    owned_here = owner_dev == rank_self
    within = block_lists - rank_self * slab_blocks
    place = ((row_reader // 32 * 2 + row_reader // 4 % 2) * 4 + row_reader // 8 % 4) * 4 + row_reader % 4
    token_iota = lax.broadcasted_iota(jnp.int32, (1, block_side, block_side), 1)
    token_map = (place[:, None, :] == token_iota).astype(jnp.bfloat16)
    place_iota = lax.broadcasted_iota(jnp.int32, (1, slab_blocks, 1), 1)
    target = owner_dev * MOST + order_rank
    slot_ids = lax.broadcasted_iota(jnp.int32, (1, devices * MOST, 1), 1)
    picker = (target[:, None, :] == slot_ids).astype(jnp.bfloat16)
    outgoing = jnp.einsum(
        "tsk,tkc->tsc", picker, teacher_logits[:, :, 0, :], preferred_element_type=jnp.float32
    ).astype(jnp.bfloat16)
    outgoing = outgoing.reshape(blocks, devices, MOST, block_side).transpose(1, 0, 2, 3)
    full, incoming = gather(hidden_states, outgoing.reshape(devices, blocks * MOST, block_side))
    gathered = full.reshape(tokens, D)
    logits = jnp.dot(gathered, head_weight, preferred_element_type=jnp.float32)
    incoming = incoming.reshape(devices, blocks, MOST, block_side)
    ordered = jnp.einsum(
        "tpj,jtmc->tmpc", token_map, incoming, preferred_element_type=jnp.float32
    ).astype(jnp.bfloat16)
    rank_iota = lax.broadcasted_iota(jnp.int32, (1, MOST, 1, 1), 1)
    hits = (
        owned_here[:, None, None, :]
        & (order_rank[:, None, None, :] == rank_iota)
        & (within[:, None, None, :] == place_iota[:, None, :, :])
    )
    choose = jnp.sum(hits.astype(jnp.int32), axis=3)
    teacher_slab = jnp.einsum(
        "tmb,tmpc->tpbc", choose.astype(jnp.bfloat16), ordered, preferred_element_type=jnp.float32
    )
    listed = jnp.sum(choose, axis=1)
    scores = logits.reshape(blocks, block_side, slab_blocks, block_side)
    listed_mask = (listed > 0)[:, None, :, None]
    local_smax = jnp.max(scores, axis=(2, 3))
    local_tmax = jnp.max(jnp.where(listed_mask, teacher_slab, -1e30), axis=(2, 3))
    local_sexp = jnp.exp(scores - local_smax[:, :, None, None])
    local_texp = jnp.exp(
        jnp.where(listed_mask, teacher_slab - local_tmax[:, :, None, None], -jnp.inf)
    )
    stat = jnp.stack(
        [
            jnp.concatenate([local_smax, local_tmax]),
            jnp.concatenate([jnp.sum(local_sexp, axis=(2, 3)), jnp.sum(local_texp, axis=(2, 3))]),
            jnp.concatenate(
                [
                    jnp.sum(jnp.where(listed_mask, 0.0, scores), axis=(2, 3)),
                    jnp.sum(local_texp * scores, axis=(2, 3)),
                ]
            ),
            jnp.concatenate(
                [jnp.zeros((blocks, block_side), jnp.float32), jnp.sum(local_texp * teacher_slab, axis=(2, 3))]
            ),
        ]
    )
    merged = stats_merge(stat)
    student_max, teacher_max = merged[0, :4], merged[0, 4:]
    student_sum, teacher_sum = merged[1, :4], merged[1, 4:]
    rest_total, cross_sum = merged[2, :4], merged[2, 4:]
    self_sum = merged[3, 4:]
    student_exp = jnp.exp(scores - student_max[:, :, None, None])
    teacher_exp = jnp.exp(
        jnp.where(listed_mask, teacher_slab - teacher_max[:, :, None, None], -jnp.inf)
    )

    def arranged(v):
        return v.reshape(blocks, N, N, 2, 4).transpose(0, 1, 3, 2, 4).reshape(blocks, block_side)

    tail_share = arranged(tail_mass)
    unlisted = float(devices * slab_width - block_side * listed_count)
    kept_mass = 1.0 - tail_share
    log_norm = student_max + jnp.log(student_sum)
    row_loss = (
        kept_mass * (jnp.log(kept_mass) - teacher_max - jnp.log(teacher_sum))
        + kept_mass * self_sum / teacher_sum
        + tail_share * jnp.log(tail_share / unlisted)
        - kept_mass * cross_sum / teacher_sum
        - tail_share / unlisted * rest_total
        + log_norm
    )
    token_loss = lax.dynamic_slice_in_dim(
        row_loss.reshape(tokens), x * block_side + (z * 2 + c) * 16 + y * 4, 4, 0
    )
    student_prob = student_exp / student_sum[:, :, None, None]
    teacher_prob = jnp.where(
        listed_mask,
        (kept_mass / teacher_sum)[:, :, None, None] * teacher_exp,
        (tail_share / unlisted)[:, :, None, None],
    )
    weight = arranged(token_weight)[:, :, None, None]
    grad_logits = (
        (weight * (student_prob - teacher_prob)).astype(jnp.bfloat16).reshape(tokens, slab_width)
    )
    grad_head = lax.dot_general(
        gathered, grad_logits, (((0,), (0,)), ((), ())), preferred_element_type=jnp.float32
    ).astype(jnp.bfloat16)
    grad_hidden = scatter(grad_logits, head_weight)
    return (token_loss, grad_head, grad_hidden)


def solution(mesh):
    split = Mesh(mesh.devices.reshape(N, N, N, 2), AXES)
    return jax.shard_map(
        on_device,
        mesh=split,
        in_specs=(P(AXES, None), P(None, AXES), P(None, None, AXES, None), P(), P(), P(), P()),
        out_specs=(P(AXES), P(None, AXES), P(AXES, None)),
        check_vma=False,
    )
```

```python
import functools

import jax
import jax.numpy as jnp
from jax import lax
from jax.experimental import pallas as pl
from jax.experimental.pallas import tpu as pltpu
from jax.sharding import Mesh
from jax.sharding import PartitionSpec as P

MOST = 4
AXES = ("x", "z", "y", "c")
N = 4
D = 5120
CHUNKS = ((0, 1280, "x", "z"), (1280, 1280, "z", "x"), (2560, 1280, "x", "z"), (3840, 1280, "z", "x"))
NC = len(CHUNKS)
DMA = pltpu.SemaphoreType.DMA
REGULAR = pltpu.SemaphoreType.REGULAR
VM = pl.BlockSpec(memory_space=pltpu.VMEM)
ANY = pl.BlockSpec(memory_space=pl.ANY)


def spot():
    return {a: lax.axis_index(a) for a in AXES}


def moved(pos, axis, step):
    if axis == "c":
        return {"c": 1 - pos["c"]}
    return {axis: lax.rem(pos[axis] + step + N, N)}


def remote(src, dst, send, recv, device):
    return pltpu.make_async_remote_copy(
        src_ref=src, dst_ref=dst, send_sem=send, recv_sem=recv,
        device_id=device, device_id_type=pl.DeviceIdType.MESH,
    )


def greet(pos, partners):
    barrier = pltpu.get_barrier_semaphore()
    for device in partners:
        pl.semaphore_signal(barrier, inc=1, device_id=device, device_id_type=pl.DeviceIdType.MESH)
    pl.semaphore_wait(barrier, len(partners))


def lines(pos, axes):
    return [moved(pos, a, s) for a in axes for s in ((1,) if a == "c" else (1, 2, 3))]


def gather_chunk(pos, f, full, asend, arecv, bsend, brecv, csend, crecv):
    start, width, A, B = CHUNKS[f]
    half = width // 2
    a, b, c = pos[A], pos[B], pos["c"]
    every, low, high = pl.ds(start, width), pl.ds(start, half), pl.ds(start + half, half)
    sent = []

    def unit(off_a, off_b, cols):
        at = {A: lax.rem(a + off_a + N, N), B: lax.rem(b + off_b + N, N)}
        return full.at[at["x"], at["z"], c, :, cols]

    def send(ref, send_sem, recv_sem, axis, step):
        copy = remote(ref, ref, send_sem, recv_sem, moved(pos, axis, step))
        copy.start()
        sent.append(copy)

    def arrived(ref, recv_sem):
        remote(ref, ref, recv_sem, recv_sem, moved(pos, "c", 1)).wait_recv()

    offs = (0, -1, 1, 2)

    def onward(j):
        ref = unit(offs[j], 0, every)
        send(ref, bsend.at[f, j, 0], brecv.at[f, j, 0], B, 1)
        send(ref, bsend.at[f, j, 1], brecv.at[f, j, 1], B, -1)
        across(j, 0)

    def across(j, k):
        send(unit(offs[j], offs[k], every), csend.at[f, j, k], crecv.at[f, j, k], "c", 1)

    ref = unit(0, 0, every)
    send(ref, asend.at[f, 0], arecv.at[f, 0], A, 1)
    send(ref, asend.at[f, 1], arecv.at[f, 1], A, -1)
    onward(0)
    yield
    arrived(unit(-1, 0, every), arecv.at[f, 0])
    send(unit(-1, 0, low), asend.at[f, 2], arecv.at[f, 2], A, 1)
    onward(1)
    arrived(unit(1, 0, every), arecv.at[f, 1])
    send(unit(1, 0, high), asend.at[f, 3], arecv.at[f, 3], A, -1)
    onward(2)
    yield

    def relay(j):
        arrived(unit(offs[j], -1, every), brecv.at[f, j, 0])
        send(unit(offs[j], -1, low), bsend.at[f, j, 2], brecv.at[f, j, 2], B, 1)
        across(j, 1)
        arrived(unit(offs[j], 1, every), brecv.at[f, j, 1])
        send(unit(offs[j], 1, high), bsend.at[f, j, 3], brecv.at[f, j, 3], B, -1)
        across(j, 2)

    relay(0)
    yield
    arrived(unit(2, 0, low), arecv.at[f, 2])
    arrived(unit(2, 0, high), arecv.at[f, 3])
    onward(3)
    yield
    relay(1)
    relay(2)
    yield
    relay(3)
    yield
    for j in range(4):
        arrived(unit(offs[j], 2, low), brecv.at[f, j, 2])
        arrived(unit(offs[j], 2, high), brecv.at[f, j, 3])
        across(j, 3)
    yield
    for j in range(4):
        for k in range(4):
            at = {A: lax.rem(a + offs[j] + N, N), B: lax.rem(b + offs[k] + N, N)}
            arrived(full.at[at["x"], at["z"], 1 - c, :, every], crecv.at[f, j, k])
    for copy in sent:
        copy.wait_send()


def run_all(gens):
    gens = list(gens)
    while gens:
        for g in list(gens):
            try:
                next(g)
            except StopIteration:
                gens.remove(g)


def plane_line(pos):
    x, z, y, c = (pos[a] for a in AXES)
    plane = [{"z": lax.rem(z + dz, N), "y": lax.rem(y + dy, N)} for dz in range(N) for dy in range(N) if dz or dy]
    line = [{"x": lax.rem(x + dx, N), "c": lax.rem(c + dc, 2)} for dx in range(N) for dc in range(2) if dx or dc]
    return plane, line


W = CHUNKS[0][1]
TILE = 256
PIECE = 512


def scatter_chunk(pos, f, gl, w, part, cs, cr, bs1, br1, bs2, br2, red, as1, ar1, ys, yr, out, csem, bsem, asem, ysem):
    start, width, A, B = CHUNKS[f]
    half = width // 2
    a, b, c, y = pos[A], pos[B], pos["c"], pos["y"]
    f32, bf16 = jnp.float32, jnp.bfloat16
    sent = []

    def index(ia, ib):
        at = {A: ia, B: ib}
        return at["x"] * N + at["z"]

    def shift(p, s):
        return lax.rem(p + s + N, N)

    def send(src, dst, sems, k, axis, step):
        copy = remote(src, dst, sems.at[0, f, k], sems.at[1, f, k], moved(pos, axis, step))
        copy.start()
        sent.append(copy)

    def arrived(ref, sems, k):
        remote(ref, ref, sems.at[0, f, k], sems.at[1, f, k], moved(pos, "c", 1)).wait_recv()

    def product(i, carry):
        rows = w[pl.ds(pl.multiple_of(start + i * TILE, TILE), TILE), :]
        got = lax.dot_general(gl[...], rows, (((1,), (1,)), ((), ())), preferred_element_type=f32)
        part[f, :, :, :, pl.ds(pl.multiple_of(i * TILE, TILE), TILE)] = got.reshape(16, 2, 16, TILE)
        return carry

    lax.fori_loop(0, width // TILE, product, 0)

    def other(u, carry):
        cs[f, u] = part[f, u, 1 - c].astype(bf16)
        return carry

    lax.fori_loop(0, 16, other, 0)
    send(cs.at[f], cr.at[f], csem, 0, "c", 1)
    yield
    arrived(cr.at[f], csem, 0)

    def chip(u):
        return part[f, u, c] + cr[f, u].astype(f32)

    def opposite(i, carry):
        v = chip(index(i, shift(b, 2))).astype(bf16)
        bs1[f, 0, i] = v[:, :half]
        bs1[f, 1, i] = v[:, half:]
        return carry

    lax.fori_loop(0, N, opposite, 0)
    send(bs1.at[f, 0], br1.at[f, 0], bsem, 0, B, 1)
    send(bs1.at[f, 1], br1.at[f, 1], bsem, 1, B, -1)
    yield
    arrived(br1.at[f, 0], bsem, 0)

    def up(i, carry):
        v = chip(index(i, shift(b, 1)))
        bs2[f, 0, i, :, :half] = (v[:, :half] + br1[f, 0, i].astype(f32)).astype(bf16)
        bs2[f, 0, i, :, half:] = v[:, half:].astype(bf16)
        return carry

    lax.fori_loop(0, N, up, 0)
    send(bs2.at[f, 0], br2.at[f, 0], bsem, 2, B, 1)
    arrived(br1.at[f, 1], bsem, 1)

    def down(i, carry):
        v = chip(index(i, shift(b, -1)))
        bs2[f, 1, i, :, :half] = v[:, :half].astype(bf16)
        bs2[f, 1, i, :, half:] = (v[:, half:] + br1[f, 1, i].astype(f32)).astype(bf16)
        return carry

    lax.fori_loop(0, N, down, 0)
    send(bs2.at[f, 1], br2.at[f, 1], bsem, 3, B, -1)
    yield
    arrived(br2.at[f, 0], bsem, 2)
    arrived(br2.at[f, 1], bsem, 3)

    def kept(i, carry):
        red[f, i] = chip(index(i, b)) + br2[f, 0, i].astype(f32) + br2[f, 1, i].astype(f32)
        return carry

    lax.fori_loop(0, N, kept, 0)
    for d in (2, 1, 3):
        as1[f, d - 1] = red[f, shift(a, d)].astype(bf16)
        send(as1.at[f, d - 1], ar1.at[f, d - 1], asem, d - 1, A, d)
    yield
    for d in (1, 2, 3):
        arrived(ar1.at[f, d - 1], asem, d - 1)
    v = red[f, a] + ar1[f, 0].astype(f32) + ar1[f, 1].astype(f32) + ar1[f, 2].astype(f32)
    for k in range(N):
        ys[f, k] = v[4 * k : 4 * k + 4, :]
    for d in (2, 1, 3):
        send(ys.at[f, shift(y, d)], yr.at[f, d - 1], ysem, d - 1, "y", d)
    yield
    for d in (1, 2, 3):
        arrived(yr.at[f, d - 1], ysem, d - 1)
    total = ys[f, y] + yr[f, 0] + yr[f, 1] + yr[f, 2]
    out[:, start : start + width] = total.astype(bf16)
    for copy in sent:
        copy.wait_send()


def step_kernel(h, tout, tmap, tcon, extra, choose, listed, w_hbm, loss, gx, gh,
                full, inc, rows, wide, w, L, gl, T32, TV, msg, near, mid, far, lmsg, lnear, lmid, lfar,
                part, cs, cr, bs1, br1, bs2, br2, red, as1, ar1, ys, yr, stage,
                wsem, ysend, yrecv, asend, arecv, bsend, brecv, csend, crecv, tsend, trecv, own, every,
                xsem, csem, bsem, asem, rsem, gsem):
    f32, bf16 = jnp.float32, jnp.bfloat16
    pos = spot()
    x, z, y, c = (pos[a] for a in AXES)
    me = ((x * N + z) * N + y) * 2 + c
    plane, line = plane_line(pos)
    loads = []
    for f, (start, width, _, _) in enumerate(CHUNKS):
        copy = pltpu.make_async_copy(w_hbm.at[pl.ds(start, width)], w.at[pl.ds(start, width)], wsem.at[f])
        copy.start()
        loads.append(copy)
    greet(pos, plane + line)

    first = []
    for d in (2, 1, 3):
        copy = remote(h, rows.at[y], ysend.at[d - 1], yrecv.at[d - 1], moved(pos, "y", d))
        copy.start()
        first.append(copy)
    mine = pltpu.make_async_copy(h, rows.at[y], own.at[0])
    mine.start()
    keep = pltpu.make_async_copy(tout.at[me], inc.at[me], own.at[1])
    keep.start()
    for device in line:
        pl.semaphore_signal(every, inc=1, device_id=device, device_id_type=pl.DeviceIdType.MESH)
    mine.wait()
    for d in (1, 2, 3):
        ref = rows.at[lax.rem(y - d + N, N)]
        remote(ref, ref, ysend.at[d - 1], yrecv.at[d - 1], moved(pos, "y", d)).wait_recv()
    for k in range(N):
        wide[4 * k : 4 * k + 4, :] = rows[k].astype(f32)
    full[x, z, c] = wide[...].astype(bf16)
    gens = [gather_chunk(pos, f, full, asend, arecv, bsend, brecv, csend, crecv) for f in range(NC)]
    for g in gens:
        next(g)
    pl.semaphore_wait(every, len(line))

    def one(k, carry):
        to = lax.rem(me + k, 128)
        device = {"x": to // 32, "z": lax.rem(to // 8, N), "y": lax.rem(to // 2, N), "c": lax.rem(to, 2)}
        remote(tout.at[to], inc.at[me], tsend, trecv, device).start()
        return carry

    lax.fori_loop(1, 128, one, 0)

    def logits_part(f, lo, hi):
        start, width = CHUNKS[f][:2]

        def tile(i, carry):
            cols = pl.ds(pl.multiple_of(i * TILE, TILE), TILE)
            got = jnp.dot(
                full[:, :, :, :, start : start + width].reshape(512, width),
                w[start : start + width, cols],
                preferred_element_type=f32,
            )
            if f == 0:
                L[:, cols] = got
            else:
                L[:, cols] += got
            return carry

        lax.fori_loop(lo, hi, tile, 0)

    def finish(g):
        for _ in g:
            pass

    g0, g1, g2, g3 = gens
    for _ in range(3):
        next(g0), next(g1)
    next(g2), next(g3)
    for _ in range(2):
        next(g0), next(g1)
        next(g2), next(g3)
    finish(g0)
    next(g2), next(g3)
    loads[0].wait()
    logits_part(0, 0, 2)
    next(g2), next(g3)
    logits_part(0, 2, 4)
    next(g2), next(g3)
    finish(g1)
    loads[1].wait()
    logits_part(1, 0, 4)
    finish(g2)
    loads[2].wait()
    logits_part(2, 0, 4)
    finish(g3)
    loads[3].wait()
    logits_part(3, 0, 4)
    for copy in first:
        copy.wait_send()

    for t in range(N):
        r = slice(128 * t, 128 * t + 128)
        top = L[r, :128]
        for b in range(1, 8):
            top = jnp.maximum(top, L[r, 128 * b : 128 * b + 128])
        col = jnp.max(top, axis=1, keepdims=True)
        acc = jnp.exp(L[r, :128] - col)
        for b in range(1, 8):
            acc = acc + jnp.exp(L[r, 128 * b : 128 * b + 128] - col)
        msg[0, t : t + 1] = jnp.max(top.T, axis=0, keepdims=True)
        msg[1, t : t + 1] = jnp.sum(acc.T, axis=0, keepdims=True)
    msg[0, 4:8] = tcon[0:4]
    msg[1, 4:8] = jnp.zeros((4, 128), f32)

    def merge(parts):
        top = parts[0][0]
        for p in parts[1:]:
            top = jnp.maximum(top, p[0])
        total = 0.0
        for p in parts:
            total += p[1] * jnp.exp(p[0] - top)
        return top, total

    for device in plane:
        remote(msg, near.at[z * N + y], xsem.at[0], xsem.at[1], device).start()
    near[z * N + y] = msg[...]

    part_inc = inc.at[pl.ds(0, 127)]
    remote(part_inc, part_inc, tsend, trecv, moved(pos, "c", 1)).wait()
    keep.wait()
    T32[...] = inc[...].reshape(2048, 128).astype(f32)

    def teacher(t):
        stored = jnp.concatenate(
            [T32[pl.ds(t * MOST + m, 128, stride=16), :] for m in range(MOST)], axis=1
        ).astype(bf16)
        ordered = jnp.dot(tmap[t], stored, preferred_element_type=f32)
        for b in range(8):
            v = choose[t * 32 + b] * ordered[:, :128]
            for m in range(1, MOST):
                v = v + choose[t * 32 + m * 8 + b] * ordered[:, 128 * m : 128 * m + 128]
            TV[t, b] = v.astype(bf16)

    teacher(0)
    teacher(1)
    group = near.at[pl.ds(0, 15)]
    remote(group, group, xsem.at[0], xsem.at[1], plane[0]).wait()
    mid[0], mid[1] = merge([near[i] for i in range(16)])
    for device in line:
        remote(mid, far.at[x * 2 + c], xsem.at[2], xsem.at[3], device).start()
    far[x * 2 + c] = mid[...]
    teacher(2)
    teacher(3)
    group = far.at[pl.ds(0, 7)]
    remote(group, group, xsem.at[2], xsem.at[3], line[0]).wait()
    top, total = merge([far[i] for i in range(8)])

    log_norm = top[0:4] + jnp.log(total[0:4])
    tail = extra[0:4]
    weight = extra[4:8]
    kept = jnp.log(1.0 - tail) - top[4:8]
    tail_prob = tail / UNLISTED
    tail_log = jnp.log(tail_prob)

    def column(v, t):
        return jnp.broadcast_to(v[t : t + 1], (128, 128)).T

    lmsg[...] = jnp.zeros((8, 128), f32)
    for t in range(N):
        r = slice(128 * t, 128 * t + 128)
        norm_c, weight_c, kept_c = column(log_norm, t), column(weight, t), column(kept, t)
        prob_c, log_c = column(tail_prob, t), column(tail_log, t)
        acc = jnp.zeros((128, 128), f32)
        for b in range(8):
            scores = L[r, 128 * b : 128 * b + 128]
            on = listed[t * 8 + b]
            off = 1.0 - on
            listed_log = TV[t, b].astype(f32) + kept_c
            q = on * jnp.exp(listed_log) + off * prob_c
            log_q = on * listed_log + off * log_c
            gap = scores - norm_c
            gl[r, 128 * b : 128 * b + 128] = (weight_c * (jnp.exp(gap) - q)).astype(bf16)
            acc = acc + q * (log_q - gap)
        lmsg[t : t + 1] = jnp.sum(acc.T, axis=0, keepdims=True)

    stores = [None, None]
    count = [0]

    def head_piece():
        i = count[0]
        if i == D // PIECE:
            return
        count[0] = i + 1
        slot = i % 2
        if stores[slot] is not None:
            stores[slot].wait()
        cols = slice(i * PIECE, i * PIECE + PIECE)

        def tile(n, carry):
            some = pl.ds(pl.multiple_of(n * TILE, TILE), TILE)
            got = lax.dot_general(
                full[:, :, :, :, cols].reshape(512, PIECE), gl[:, some], (((0,), (0,)), ((), ())),
                preferred_element_type=f32,
            )
            stage[slot, :, some] = got.astype(bf16)
            return carry

        lax.fori_loop(0, 1024 // TILE, tile, 0)
        stores[slot] = pltpu.make_async_copy(stage.at[slot], gh.at[pl.ds(i * PIECE, PIECE)], gsem.at[slot])
        stores[slot].start()

    s0, s1, s2, s3 = [
        scatter_chunk(pos, f, gl, w, part, cs, cr, bs1, br1, bs2, br2, red, as1, ar1, ys, yr, gx, csem, bsem, asem, rsem)
        for f in range(NC)
    ]
    next(s0)
    next(s1)
    next(s0)
    next(s2)
    next(s1)
    next(s3)
    next(s0)
    next(s2)
    next(s1)
    next(s3)
    for device in plane:
        remote(lmsg, lnear.at[z * N + y], xsem.at[4], xsem.at[5], device).start()
    lnear[z * N + y] = lmsg[...]
    head_piece()
    head_piece()
    next(s0)
    next(s1)
    head_piece()
    next(s2)
    next(s3)
    group = lnear.at[pl.ds(0, 15)]
    remote(group, group, xsem.at[4], xsem.at[5], plane[0]).wait()
    total = lnear[0]
    for i in range(1, 16):
        total = total + lnear[i]
    lmid[...] = total
    for device in line:
        remote(lmid, lfar.at[x * 2 + c], xsem.at[6], xsem.at[7], device).start()
    lfar[x * 2 + c] = lmid[...]
    head_piece()
    next(s0)
    next(s1)
    head_piece()
    head_piece()
    next(s2)
    next(s3)
    head_piece()
    finish(s0)
    finish(s1)
    head_piece()
    next(s2)
    next(s3)
    head_piece()
    head_piece()
    group = lfar.at[pl.ds(0, 7)]
    remote(group, group, xsem.at[6], xsem.at[7], line[0]).wait()
    total = lfar[0]
    for i in range(1, 8):
        total = total + lfar[i]
    loss[...] = total
    finish(s2)
    finish(s3)
    for copy in stores:
        copy.wait()


UNLISTED = 98304.0


def step(hidden, outgoing, token_map, own_norm, extra, choose, listed, head):
    bf16, f32 = jnp.bfloat16, jnp.float32
    half = W // 2
    V = pltpu.VMEM
    SM = pl.BlockSpec(memory_space=pltpu.SMEM)
    return pl.pallas_call(
        step_kernel,
        out_shape=(
            jax.ShapeDtypeStruct((8, 128), f32),
            jax.ShapeDtypeStruct((4, D), bf16),
            jax.ShapeDtypeStruct(head.shape, bf16),
        ),
        in_specs=[VM, VM, VM, VM, VM, SM, SM, ANY],
        out_specs=(VM, VM, ANY),
        scratch_shapes=[
            V((N, N, 2, 16, D), bf16),
            V((128, 16, 128), bf16),
            V((N, 4, D), bf16),
            V((16, D), f32),
            V(head.shape, bf16),
            V((512, 1024), f32),
            V((512, 1024), bf16),
            V((2048, 128), f32),
            V((N, 8, 128, 128), bf16),
            V((2, 8, 128), f32), V((16, 2, 8, 128), f32), V((2, 8, 128), f32), V((8, 2, 8, 128), f32),
            V((8, 128), f32), V((16, 8, 128), f32), V((8, 128), f32), V((8, 8, 128), f32),
            V((NC, 16, 2, 16, W), f32),
            V((NC, 16, 16, W), bf16), V((NC, 16, 16, W), bf16),
            V((NC, 2, N, 16, half), bf16), V((NC, 2, N, 16, half), bf16),
            V((NC, 2, N, 16, W), bf16), V((NC, 2, N, 16, W), bf16),
            V((NC, N, 16, W), f32),
            V((NC, 3, 16, W), bf16), V((NC, 3, 16, W), bf16),
            V((NC, N, 4, W), f32), V((NC, 3, 4, W), f32),
            V((2, PIECE, 1024), bf16),
            DMA((NC,)),
            DMA((3,)), DMA((3,)),
            DMA((NC, 4)), DMA((NC, 4)),
            DMA((NC, 4, 4)), DMA((NC, 4, 4)),
            DMA((NC, 4, 4)), DMA((NC, 4, 4)),
            DMA, DMA, DMA((2,)), REGULAR,
            DMA((8,)),
            DMA((2, NC, 1)), DMA((2, NC, 4)), DMA((2, NC, 3)), DMA((2, NC, 3)), DMA((2,)),
        ],
        compiler_params=pltpu.CompilerParams(collective_id=0, has_side_effects=True, vmem_limit_bytes=67043328),
        name="step",
    )(hidden, outgoing, token_map, own_norm, extra, choose, listed, head)


def on_device(
    hidden_states, head_weight, teacher_logits, block_lists, row_reader, tail_mass, token_weight
):
    blocks, listed_count, stored_rows, block_side = teacher_logits.shape
    slab_width = head_weight.shape[1]
    slab_blocks = slab_width // block_side
    devices = 128
    x, z, y, c = (lax.axis_index(a) for a in AXES)
    rank_self = ((x * N + z) * N + y) * 2 + c
    owner_dev = block_lists // slab_blocks
    earlier = lax.broadcasted_iota(
        jnp.int32, (1, listed_count, listed_count), 2
    ) < lax.broadcasted_iota(jnp.int32, (1, listed_count, listed_count), 1)
    same_owner = owner_dev[:, :, None] == owner_dev[:, None, :]
    order_rank = jnp.sum((same_owner & earlier).astype(jnp.int32), axis=2)
    owned_here = owner_dev == rank_self
    within = block_lists - rank_self * slab_blocks
    place = ((row_reader // 32 * 2 + row_reader // 4 % 2) * 4 + row_reader // 8 % 4) * 4 + row_reader % 4
    token_iota = lax.broadcasted_iota(jnp.int32, (1, block_side, block_side), 1)
    token_map = (place[:, None, :] == token_iota).astype(jnp.bfloat16)
    place_iota = lax.broadcasted_iota(jnp.int32, (1, slab_blocks, 1), 1)
    target = owner_dev * MOST + order_rank
    slot_ids = lax.broadcasted_iota(jnp.int32, (1, devices * MOST, 1), 1)
    picker = (target[:, None, :] == slot_ids).astype(jnp.bfloat16)
    outgoing = jnp.einsum(
        "tsk,tkc->tsc", picker, teacher_logits[:, :, 0, :], preferred_element_type=jnp.float32
    ).astype(jnp.bfloat16)
    outgoing = outgoing.reshape(blocks, devices, MOST, block_side).transpose(1, 0, 2, 3)
    outgoing = outgoing.reshape(devices, blocks * MOST, block_side)
    rank_iota = lax.broadcasted_iota(jnp.int32, (1, MOST, 1, 1), 1)
    hits = (
        owned_here[:, None, None, :]
        & (order_rank[:, None, None, :] == rank_iota)
        & (within[:, None, None, :] == place_iota[:, None, :, :])
    )
    choose = jnp.sum(hits.astype(jnp.float32), axis=3)
    listed = jnp.sum(choose, axis=1)
    stored = teacher_logits[:, :, 0, :].astype(jnp.float32)
    stored_max = jnp.max(stored, axis=(1, 2))
    stored_norm = stored_max + jnp.log(jnp.sum(jnp.exp(stored - stored_max[:, None, None]), axis=(1, 2)))
    lane = lax.broadcasted_iota(jnp.int32, (blocks, block_side), 1)
    mine = lax.dynamic_slice_in_dim(place, rank_self, 1, 1)
    own_norm = jnp.where(lane == mine, stored_norm[:, None], -1e30)

    def arranged(v):
        return v.reshape(blocks, N, N, 2, 4).transpose(0, 1, 3, 2, 4).reshape(blocks, block_side)

    extra = jnp.concatenate([arranged(tail_mass), arranged(token_weight)])
    row_loss, grad_hidden, grad_head = step(
        hidden_states, outgoing, token_map, own_norm, extra, choose.reshape(-1), listed.reshape(-1), head_weight
    )
    token_loss = lax.dynamic_slice(row_loss, (x, (z * 2 + c) * 16 + y * 4), (1, 4)).reshape(4)
    return (token_loss, grad_head, grad_hidden)


def solution(mesh):
    split = Mesh(mesh.devices.reshape(N, N, N, 2), AXES)
    return jax.shard_map(
        on_device,
        mesh=split,
        in_specs=(P(AXES, None), P(None, AXES), P(None, None, AXES, None), P(), P(), P(), P()),
        out_specs=(P(AXES), P(None, AXES), P(AXES, None)),
        check_vma=False,
    )
```

```python
import functools

import jax
import jax.numpy as jnp
from jax import lax
from jax.experimental import pallas as pl
from jax.experimental.pallas import tpu as pltpu
from jax.sharding import Mesh
from jax.sharding import PartitionSpec as P

MOST = 4
AXES = ("x", "z", "y", "c")
N = 4
D = 5120
CHUNKS = ((0, 1280, "x", "z"), (1280, 1280, "z", "x"), (2560, 1280, "x", "z"), (3840, 1280, "z", "x"))
NC = len(CHUNKS)
DMA = pltpu.SemaphoreType.DMA
REGULAR = pltpu.SemaphoreType.REGULAR
VM = pl.BlockSpec(memory_space=pltpu.VMEM)
ANY = pl.BlockSpec(memory_space=pl.ANY)


def spot():
    return {a: lax.axis_index(a) for a in AXES}


def moved(pos, axis, step):
    if axis == "c":
        return {"c": 1 - pos["c"]}
    return {axis: lax.rem(pos[axis] + step + N, N)}


def remote(src, dst, send, recv, device):
    return pltpu.make_async_remote_copy(
        src_ref=src, dst_ref=dst, send_sem=send, recv_sem=recv,
        device_id=device, device_id_type=pl.DeviceIdType.MESH,
    )


def greet(pos, partners):
    barrier = pltpu.get_barrier_semaphore()
    for device in partners:
        pl.semaphore_signal(barrier, inc=1, device_id=device, device_id_type=pl.DeviceIdType.MESH)
    pl.semaphore_wait(barrier, len(partners))


def lines(pos, axes):
    return [moved(pos, a, s) for a in axes for s in ((1,) if a == "c" else (1, 2, 3))]


def gather_chunk(pos, f, full, asend, arecv, bsend, brecv, csend, crecv):
    start, width, A, B = CHUNKS[f]
    half = width // 2
    a, b, c = pos[A], pos[B], pos["c"]
    every, low, high = pl.ds(start, width), pl.ds(start, half), pl.ds(start + half, half)
    sent = []

    def unit(off_a, off_b, cols):
        at = {A: lax.rem(a + off_a + N, N), B: lax.rem(b + off_b + N, N)}
        return full.at[at["x"], at["z"], c, :, cols]

    def send(ref, send_sem, recv_sem, axis, step):
        copy = remote(ref, ref, send_sem, recv_sem, moved(pos, axis, step))
        copy.start()
        sent.append(copy)

    def arrived(ref, recv_sem):
        remote(ref, ref, recv_sem, recv_sem, moved(pos, "c", 1)).wait_recv()

    offs = (0, -1, 1, 2)

    def onward(j):
        ref = unit(offs[j], 0, every)
        send(ref, bsend.at[f, j, 0], brecv.at[f, j, 0], B, 1)
        send(ref, bsend.at[f, j, 1], brecv.at[f, j, 1], B, -1)
        across(j, 0)

    def across(j, k):
        send(unit(offs[j], offs[k], every), csend.at[f, j, k], crecv.at[f, j, k], "c", 1)

    ref = unit(0, 0, every)
    send(ref, asend.at[f, 0], arecv.at[f, 0], A, 1)
    send(ref, asend.at[f, 1], arecv.at[f, 1], A, -1)
    onward(0)
    yield
    arrived(unit(-1, 0, every), arecv.at[f, 0])
    send(unit(-1, 0, low), asend.at[f, 2], arecv.at[f, 2], A, 1)
    onward(1)
    arrived(unit(1, 0, every), arecv.at[f, 1])
    send(unit(1, 0, high), asend.at[f, 3], arecv.at[f, 3], A, -1)
    onward(2)
    yield

    def relay(j):
        arrived(unit(offs[j], -1, every), brecv.at[f, j, 0])
        send(unit(offs[j], -1, low), bsend.at[f, j, 2], brecv.at[f, j, 2], B, 1)
        across(j, 1)
        arrived(unit(offs[j], 1, every), brecv.at[f, j, 1])
        send(unit(offs[j], 1, high), bsend.at[f, j, 3], brecv.at[f, j, 3], B, -1)
        across(j, 2)

    relay(0)
    yield
    arrived(unit(2, 0, low), arecv.at[f, 2])
    arrived(unit(2, 0, high), arecv.at[f, 3])
    onward(3)
    yield
    relay(1)
    relay(2)
    yield
    relay(3)
    yield
    for j in range(4):
        arrived(unit(offs[j], 2, low), brecv.at[f, j, 2])
        arrived(unit(offs[j], 2, high), brecv.at[f, j, 3])
        across(j, 3)
    yield
    for j in range(4):
        for k in range(4):
            at = {A: lax.rem(a + offs[j] + N, N), B: lax.rem(b + offs[k] + N, N)}
            arrived(full.at[at["x"], at["z"], 1 - c, :, every], crecv.at[f, j, k])
    for copy in sent:
        copy.wait_send()


def run_all(gens):
    gens = list(gens)
    while gens:
        for g in list(gens):
            try:
                next(g)
            except StopIteration:
                gens.remove(g)


def plane_line(pos):
    x, z, y, c = (pos[a] for a in AXES)
    plane = [{"z": lax.rem(z + dz, N), "y": lax.rem(y + dy, N)} for dz in range(N) for dy in range(N) if dz or dy]
    line = [{"x": lax.rem(x + dx, N), "c": lax.rem(c + dc, 2)} for dx in range(N) for dc in range(2) if dx or dc]
    return plane, line


SCATTER = (
    (0, 1280, "x", "z"), (1280, 1280, "z", "x"), (2560, 1280, "x", "z"), (3840, 1280, "z", "x"),
)
NS = len(SCATTER)
W = 1280
TILE = 256
OFF = (0, 1, 3, 5)
FILL = {3: 2, 4: 2, 5: 2, 6: 2, 7: 2}
PIECE = 512


def scatter_chunk(pos, f, gl, w, part, cs, cr, bs, br, keep, ps, pr, out, csem, bsem, psend, precv):
    start, width, A, B = SCATTER[f]
    a, b, c, y = pos[A], pos[B], pos["c"], pos["y"]
    f32, bf16 = jnp.float32, jnp.bfloat16
    part = part.at[f, :, :, :width]
    cs, cr = cs.at[f, :, :, :width], cr.at[f, :, :, :width]
    bs, br = bs.at[f, :, :, :, :width], br.at[f, :, :, :, :width]
    keep, ps, pr = keep.at[f, :, :, :width], ps.at[f, :, :, :, :width], pr.at[f, :, :, :width]
    sent = []

    def index(ia, ib):
        at = {A: ia, B: ib}
        return at["x"] * N + at["z"]

    def shift(p, s):
        return lax.rem(p + s + N, N)

    def send(src, dst, ssem, rsem, device):
        copy = remote(src, dst, ssem, rsem, device)
        copy.start()
        sent.append(copy)

    def arrived(ref, rsem):
        remote(ref, ref, rsem, rsem, moved(pos, "c", 1)).wait_recv()

    def product(i, carry):
        rows = w[pl.ds(pl.multiple_of(start + i * TILE, TILE), TILE), :]
        got = lax.dot_general(
            gl[...].reshape(512, 1024), rows, (((1,), (1,)), ((), ())), preferred_element_type=f32
        )
        some = pl.ds(pl.multiple_of(i * TILE, TILE), TILE)
        cs[:, :, some] = got[:256].reshape(16, 16, TILE).astype(bf16)
        part[:, :, some] = got[256:].reshape(16, 16, TILE)
        return carry

    lax.fori_loop(0, width // TILE, product, 0)
    send(cs, cr, csem.at[0, f], csem.at[1, f], moved(pos, "c", 1))
    yield
    arrived(cr, csem.at[1, f])

    def chip(u):
        return part[u] + cr[u].astype(f32)

    for d in (2, 1, 3):
        def sums(i, carry):
            bs[d - 1, i] = chip(index(i, shift(b, d))).astype(bf16)
            return carry

        lax.fori_loop(0, N, sums, 0)
        send(bs.at[d - 1], br.at[d - 1], bsem.at[0, f, d - 1], bsem.at[1, f, d - 1], moved(pos, B, d))
    yield
    for d in (1, 2, 3):
        arrived(br.at[d - 1], bsem.at[1, f, d - 1])
    for da in (2, 1, 3, 0):
        to = shift(a, da)
        v = chip(index(to, b)) + br[0, to].astype(f32) + br[1, to].astype(f32) + br[2, to].astype(f32)
        for k in range(N):
            ps[da, k] = v[4 * k : 4 * k + 4, :].astype(bf16)
            if da == 0:
                keep[k] = v[4 * k : 4 * k + 4, :]
        for dy in (2, 1, 3, 0):
            if da or dy:
                device = {A: to, "y": shift(y, dy)}
                slot = a * N + y
                send(ps.at[da, shift(y, dy)], pr.at[slot], psend.at[f], precv.at[f], device)
    yield
    group = pr.at[pl.ds(0, 15)]
    arrived(group, precv.at[f])
    mine = a * N + y
    total = keep[y]
    for d in range(1, 16):
        total = total + pr[lax.rem(mine + d, 16)].astype(f32)
    out[:, start : start + width] = total.astype(bf16)
    for copy in sent:
        copy.wait_send()


def step_kernel(h, tl, bl, rr, given, w_hbm, loss, gx, gh,
                tout, tmap, tcon, extra, CH, full, inc, rows, wide, w, L, gl, far_gl, T32, TV, msg, near, mid, far, lmsg, lnear, lmid, lfar,
                part, cs, cr, bs, br, kept_rows, ps, pr, stage,
                wsem, ysend, yrecv, asend, arecv, bsend, brecv, csend, crecv, tsend, trecv, own, zsem, every, pair,
                xsem, rcsem, rbsem, psend, precv, gsem):
    f32, bf16 = jnp.float32, jnp.bfloat16
    pos = spot()
    x, z, y, c = (pos[a] for a in AXES)
    me = ((x * N + z) * N + y) * 2 + c
    plane, line = plane_line(pos)
    loads = []
    for f, (start, width, _, _) in enumerate(CHUNKS):
        copy = pltpu.make_async_copy(w_hbm.at[pl.ds(start, width)], w.at[pl.ds(start, width)], wsem.at[f])
        copy.start()
        loads.append(copy)
    greet(pos, lines(pos, AXES))

    first = []
    for f, (start, width, _, _) in enumerate(CHUNKS):
        cols = pl.ds(start, width)
        for d in (2, 1, 3):
            copy = remote(
                h.at[:, cols], rows.at[y, :, cols], ysend.at[f, d - 1], yrecv.at[f, d - 1], moved(pos, "y", d)
            )
            copy.start()
            first.append(copy)
    for device in lines(pos, ("z",)):
        pl.semaphore_signal(zsem, inc=1, device_id=device, device_id_type=pl.DeviceIdType.MESH)
    rows[y] = h[...]

    def iota(shape, axis):
        return lax.broadcasted_iota(jnp.int32, shape, axis)

    stored = rr[...]
    place = (((stored >> 5) * 2 + ((stored >> 2) & 1)) * 4 + ((stored >> 3) & 3)) * 4 + (stored & 3)
    lane = iota((4, 128), 1)
    mine = jnp.sum(jnp.where(lane == me, place.astype(f32), 0.0), axis=1, keepdims=True)
    here = lane.astype(f32) == mine

    def norms(t):
        v = tl[t].astype(f32)
        top = jnp.max(jnp.max(v, axis=0, keepdims=True), axis=1, keepdims=True)
        total = jnp.sum(jnp.sum(jnp.exp(v - top), axis=0, keepdims=True), axis=1, keepdims=True)
        tcon[t : t + 1] = jnp.where(here[t : t + 1], top + jnp.log(total), -1e30)
        at = jnp.broadcast_to(place[t : t + 1], (128, 128))
        tmap[t] = jnp.where(iota((128, 128), 0) == at, 1.0, 0.0).astype(bf16)

    def slots(t):
        lists = bl[t : t + 1]
        owner = lists >> 3
        held = jnp.where(iota((128, 256), 0) == owner, 1.0, 0.0)
        before = jnp.where(iota((256, 256), 0) < iota((256, 256), 1), 1.0, 0.0).astype(bf16)
        seen = jnp.dot(held.astype(bf16), before, preferred_element_type=f32)
        rank = jnp.sum(held * seen, axis=0, keepdims=True).astype(jnp.int32)
        pick = jnp.where(iota((512, 256), 0) == rank * 128 + owner, 1.0, 0.0).astype(bf16)
        got = jnp.dot(pick, tl[t], preferred_element_type=f32)
        for m in range(MOST):
            T32[pl.ds(t * MOST + m, 128, stride=16), :] = got[128 * m : 128 * m + 128]
        local = jnp.where(owner == me, rank * 8 + (lists & 7), -1)
        kept = jnp.sum(jnp.where(iota((32, 256), 0) == local, 1.0, 0.0), axis=1, keepdims=True)
        CH[t] = jnp.broadcast_to(kept, (32, 128))

    norms(0)
    norms(1)
    gens = []
    for f, (start, width, _, _) in enumerate(CHUNKS):
        cols = pl.ds(start, width)
        for d in (1, 2, 3):
            ref = rows.at[lax.rem(y - d + N, N), :, cols]
            remote(ref, ref, ysend.at[f, d - 1], yrecv.at[f, d - 1], moved(pos, "y", d)).wait_recv()
        for k in range(N):
            wide[4 * k : 4 * k + 4, cols] = rows[k, :, cols].astype(f32)
        full[x, z, c, :, cols] = wide[:, cols].astype(bf16)
        g = gather_chunk(pos, f, full, asend, arecv, bsend, brecv, csend, crecv)
        next(g)
        gens.append(g)
    slots(0)
    slots(1)
    pl.semaphore_wait(zsem, 3)
    for device in lines(pos, ("x",)):
        pl.semaphore_signal(every, inc=1, device_id=device, device_id_type=pl.DeviceIdType.MESH)

    def one(k, carry):
        to = lax.rem(me + k, 128)
        device = {"x": to // 32, "z": lax.rem(to // 8, N), "y": lax.rem(to // 2, N), "c": lax.rem(to, 2)}
        remote(tout.at[to], inc.at[me], tsend, trecv, device).start()
        return carry

    def logits_part(f, lo, hi):
        start, width = CHUNKS[f][:2]

        def tile(i, carry):
            cols = pl.ds(pl.multiple_of(i * TILE, TILE), TILE)
            got = jnp.dot(
                full[:, :, :, :, start : start + width].reshape(512, width),
                w[start : start + width, cols],
                preferred_element_type=f32,
            )
            if f == 0:
                L[:, cols] = got
            else:
                L[:, cols] += got
            return carry

        lax.fori_loop(lo, hi, tile, 0)

    def finish(g):
        for _ in g:
            pass

    g0, g1, g2, g3 = gens
    next(g0), next(g1)
    next(g2), next(g3)
    slots(2)
    next(g0), next(g1)
    slots(3)
    next(g2), next(g3)
    norms(2)
    norms(3)
    pl.semaphore_wait(every, 3)
    pl.semaphore_signal(pair, inc=1, device_id=moved(pos, "c", 1), device_id_type=pl.DeviceIdType.MESH)
    next(g0), next(g1)
    tout[...] = T32[...].reshape(128, 16, 128).astype(bf16)
    keep = pltpu.make_async_copy(tout.at[me], inc.at[me], own.at[0])
    keep.start()
    pl.semaphore_wait(pair, 1)
    next(g2), next(g3)
    next(g0), next(g1)
    natural = iota((128, 128), 1)
    natural = (natural >> 5) * 32 + ((natural >> 2) & 3) * 8 + ((natural >> 4) & 1) * 4 + (natural & 3)
    turn = jnp.where(iota((128, 128), 0) == natural, 1.0, 0.0)
    extra[...] = jnp.dot(given[...], turn, preferred_element_type=f32, precision=lax.Precision.HIGHEST)
    next(g2), next(g3)
    next(g0), next(g1)
    finish(g0)
    next(g2), next(g3)
    loads[0].wait()
    logits_part(0, 0, 2)
    next(g2), next(g3)
    lax.fori_loop(1, 128, one, 0)
    logits_part(0, 2, 4)
    finish(g1)
    loads[1].wait()
    logits_part(1, 0, 4)
    finish(g2)
    loads[2].wait()
    logits_part(2, 0, 4)
    finish(g3)
    loads[3].wait()
    logits_part(3, 0, 4)
    for copy in first:
        copy.wait_send()

    for t in range(N):
        r = slice(128 * t, 128 * t + 128)
        top = L[r, :128]
        for b in range(1, 8):
            top = jnp.maximum(top, L[r, 128 * b : 128 * b + 128])
        col = jnp.max(top, axis=1, keepdims=True)
        acc = jnp.exp(L[r, :128] - col)
        for b in range(1, 8):
            acc = acc + jnp.exp(L[r, 128 * b : 128 * b + 128] - col)
        msg[0, t : t + 1] = jnp.max(top.T, axis=0, keepdims=True)
        msg[1, t : t + 1] = jnp.sum(acc.T, axis=0, keepdims=True)
    msg[0, 4:8] = tcon[0:4]
    msg[1, 4:8] = jnp.zeros((4, 128), f32)

    def merge(parts):
        top = parts[0][0]
        for p in parts[1:]:
            top = jnp.maximum(top, p[0])
        total = 0.0
        for p in parts:
            total += p[1] * jnp.exp(p[0] - top)
        return top, total

    for device in plane:
        remote(msg, near.at[z * N + y], xsem.at[0], xsem.at[1], device).start()
    near[z * N + y] = msg[...]

    part_inc = inc.at[pl.ds(0, 127)]
    remote(part_inc, part_inc, tsend, trecv, moved(pos, "c", 1)).wait()
    keep.wait()
    T32[...] = inc[...].reshape(2048, 128).astype(f32)

    def teacher(t):
        stored = jnp.concatenate(
            [T32[pl.ds(t * MOST + m, 128, stride=16), :] for m in range(MOST)], axis=1
        ).astype(bf16)
        ordered = jnp.dot(tmap[t], stored, preferred_element_type=f32)
        for b in range(8):
            v = CH[t, b : b + 1] * ordered[:, :128]
            for m in range(1, MOST):
                v = v + CH[t, m * 8 + b : m * 8 + b + 1] * ordered[:, 128 * m : 128 * m + 128]
            TV[t, b] = v.astype(bf16)

    teacher(0)
    teacher(1)
    group = near.at[pl.ds(0, 15)]
    remote(group, group, xsem.at[0], xsem.at[1], plane[0]).wait()
    mid[0], mid[1] = merge([near[i] for i in range(16)])
    for device in line:
        remote(mid, far.at[x * 2 + c], xsem.at[2], xsem.at[3], device).start()
    far[x * 2 + c] = mid[...]
    teacher(2)
    teacher(3)
    group = far.at[pl.ds(0, 7)]
    remote(group, group, xsem.at[2], xsem.at[3], line[0]).wait()
    top, total = merge([far[i] for i in range(8)])

    log_norm = top[0:4] + jnp.log(total[0:4])
    tail = extra[0:4]
    weight = extra[4:8]
    kept = jnp.log(1.0 - tail) - top[4:8]
    tail_prob = tail / UNLISTED
    tail_log = jnp.log(tail_prob)

    def column(v, t):
        return jnp.broadcast_to(v[t : t + 1], (128, 128)).T

    lmsg[...] = jnp.zeros((8, 128), f32)
    for t in range(N):
        r = slice(128 * t, 128 * t + 128)
        norm_c, weight_c, kept_c = column(log_norm, t), column(weight, t), column(kept, t)
        prob_c, log_c = column(tail_prob, t), column(tail_log, t)
        acc = jnp.zeros((128, 128), f32)
        for b in range(8):
            scores = L[r, 128 * b : 128 * b + 128]
            on = CH[t, b : b + 1] + CH[t, 8 + b : 9 + b] + CH[t, 16 + b : 17 + b] + CH[t, 24 + b : 25 + b]
            off = 1.0 - on
            listed_log = TV[t, b].astype(f32) + kept_c
            q = on * jnp.exp(listed_log) + off * prob_c
            log_q = on * listed_log + off * log_c
            gap = scores - norm_c
            g = (weight_c * (jnp.exp(gap) - q)).astype(bf16)
            gl[r, 128 * b : 128 * b + 128] = g
            g = g.reshape(4, 2, 16, 128)
            far_gl[c, 4 * t : 4 * t + 4, :, 128 * b : 128 * b + 128] = g[:, 1]
            far_gl[1 - c, 4 * t : 4 * t + 4, :, 128 * b : 128 * b + 128] = g[:, 0]
            acc = acc + q * (log_q - gap)
        lmsg[t : t + 1] = jnp.sum(acc.T, axis=0, keepdims=True)

    stores = [None, None]
    count = [0]

    def head_pieces(n):
        lo = count[0]
        count[0] = lo + n

        def piece(i, carry):
            some = pl.ds(pl.multiple_of(i * PIECE, PIECE), PIECE)
            gh[some, :] = lax.dot_general(
                full[:, :, :, :, some].reshape(512, PIECE), gl[...], (((0,), (0,)), ((), ())),
                preferred_element_type=f32,
            ).astype(bf16)
            return carry

        lax.fori_loop(lo, lo + n, piece, 0)

    chunks = [
        scatter_chunk(pos, f, far_gl, w, part, cs, cr, bs, br, kept_rows, ps, pr, gx, rcsem, rbsem, psend, precv)
        for f in range(NS)
    ]
    for tick in range(NS + OFF[-1]):
        for f in range(NS):
            if tick - f in OFF:
                next(chunks[f], None)
        if tick == 0:
            for device in plane:
                remote(lmsg, lnear.at[z * N + y], xsem.at[4], xsem.at[5], device).start()
            lnear[z * N + y] = lmsg[...]
        if tick == OFF[1] + 3:
            group = lnear.at[pl.ds(0, 15)]
            remote(group, group, xsem.at[4], xsem.at[5], plane[0]).wait()
            total = lnear[0]
            for i in range(1, 16):
                total = total + lnear[i]
            lmid[...] = total
            for device in line:
                remote(lmid, lfar.at[x * 2 + c], xsem.at[6], xsem.at[7], device).start()
            lfar[x * 2 + c] = lmid[...]
        if tick in FILL:
            head_pieces(FILL[tick])
    group = lfar.at[pl.ds(0, 7)]
    remote(group, group, xsem.at[6], xsem.at[7], line[0]).wait()
    total = lfar[0]
    for i in range(1, 8):
        total = total + lfar[i]
    loss[...] = total


UNLISTED = 98304.0


def step(hidden, teacher, lists, reader, given, head):
    bf16, f32 = jnp.bfloat16, jnp.float32
    V = pltpu.VMEM
    return pl.pallas_call(
        step_kernel,
        out_shape=(
            jax.ShapeDtypeStruct((8, 128), f32),
            jax.ShapeDtypeStruct((4, D), bf16),
            pltpu.VMEM(head.shape, bf16),
        ),
        in_specs=[VM, VM, VM, VM, VM, ANY],
        out_specs=(VM, VM, VM),
        scratch_shapes=[
            V((128, 16, 128), bf16), V((N, 128, 128), bf16), V((N, 128), f32), V((8, 128), f32), V((N, 32, 128), f32),
            V((N, N, 2, 16, D), bf16),
            V((128, 16, 128), bf16),
            V((N, 4, D), bf16),
            V((16, D), f32),
            V(head.shape, bf16),
            V((512, 1024), f32),
            V((512, 1024), bf16),
            V((2, 16, 16, 1024), bf16),
            V((2048, 128), f32),
            V((N, 8, 128, 128), bf16),
            V((2, 8, 128), f32), V((16, 2, 8, 128), f32), V((2, 8, 128), f32), V((8, 2, 8, 128), f32),
            V((8, 128), f32), V((16, 8, 128), f32), V((8, 128), f32), V((8, 8, 128), f32),
            V((NS, 16, 16, W), f32),
            V((NS, 16, 16, W), bf16), V((NS, 16, 16, W), bf16),
            V((NS, 3, N, 16, W), bf16), V((NS, 3, N, 16, W), bf16),
            V((NS, N, 4, W), f32),
            V((NS, N, N, 4, W), bf16), V((NS, 16, 4, W), bf16),
            V((8, 128), bf16),
            DMA((NC,)),
            DMA((NC, 3)), DMA((NC, 3)),
            DMA((NC, 4)), DMA((NC, 4)),
            DMA((NC, 4, 4)), DMA((NC, 4, 4)),
            DMA((NC, 4, 4)), DMA((NC, 4, 4)),
            DMA, DMA, DMA((2,)), REGULAR, REGULAR, REGULAR,
            DMA((8,)),
            DMA((2, NS)), DMA((2, NS, 3)), DMA((NS,)), DMA((NS,)), DMA((2,)),
        ],
        compiler_params=pltpu.CompilerParams(collective_id=0, has_side_effects=True, vmem_limit_bytes=53 << 20),
        name="step",
    )(hidden, teacher, lists, reader, given, head)


def on_device(
    hidden_states, head_weight, teacher_logits, block_lists, row_reader, tail_mass, token_weight
):
    x, z, y, c = (lax.axis_index(a) for a in AXES)
    given = jnp.concatenate([tail_mass.reshape(N, 128), token_weight.reshape(N, 128)])
    row_loss, grad_hidden, grad_head = step(
        hidden_states, teacher_logits[:, :, 0, :], block_lists, row_reader, given, head_weight
    )
    token_loss = lax.dynamic_slice(row_loss, (x, (z * 2 + c) * 16 + y * 4), (1, 4)).reshape(4)
    return (token_loss, grad_head, grad_hidden)


def solution(mesh):
    split = Mesh(mesh.devices.reshape(N, N, N, 2), AXES)
    return jax.shard_map(
        on_device,
        mesh=split,
        in_specs=(P(AXES, None), P(None, AXES), P(None, None, AXES, None), P(), P(), P(), P()),
        out_specs=(P(AXES), P(None, AXES), P(AXES, None)),
        check_vma=False,
    )
```

```python
import functools

import jax
import jax.numpy as jnp
from jax import lax
from jax.experimental import pallas as pl
from jax.experimental.pallas import tpu as pltpu
from jax.sharding import Mesh
from jax.sharding import PartitionSpec as P

MOST = 4
AXES = ("x", "z", "y", "c")
N = 4
D = 5120
CHUNKS = ((0, 1280, "x", "z"), (1280, 1280, "z", "x"), (2560, 1280, "x", "z"), (3840, 1280, "z", "x"))
NC = len(CHUNKS)
DMA = pltpu.SemaphoreType.DMA
REGULAR = pltpu.SemaphoreType.REGULAR
VM = pl.BlockSpec(memory_space=pltpu.VMEM)
ANY = pl.BlockSpec(memory_space=pl.ANY)


def spot():
    return {a: lax.axis_index(a) for a in AXES}


def moved(pos, axis, step):
    if axis == "c":
        return {"c": 1 - pos["c"]}
    return {axis: lax.rem(pos[axis] + step + N, N)}


def remote(src, dst, send, recv, device):
    return pltpu.make_async_remote_copy(
        src_ref=src, dst_ref=dst, send_sem=send, recv_sem=recv,
        device_id=device, device_id_type=pl.DeviceIdType.MESH,
    )


def greet(pos, partners):
    barrier = pltpu.get_barrier_semaphore()
    for device in partners:
        pl.semaphore_signal(barrier, inc=1, device_id=device, device_id_type=pl.DeviceIdType.MESH)
    pl.semaphore_wait(barrier, len(partners))


def lines(pos, axes):
    return [moved(pos, a, s) for a in axes for s in ((1,) if a == "c" else (1, 2, 3))]


def gather_chunk(pos, f, full, asend, arecv, bsend, brecv, csend, crecv):
    start, width, A, B = CHUNKS[f]
    half = width // 2
    a, b, c = pos[A], pos[B], pos["c"]
    every, low, high = pl.ds(start, width), pl.ds(start, half), pl.ds(start + half, half)
    sent = []

    def unit(off_a, off_b, cols):
        at = {A: lax.rem(a + off_a + N, N), B: lax.rem(b + off_b + N, N)}
        return full.at[at["x"], at["z"], c, :, cols]

    def send(ref, send_sem, recv_sem, axis, step):
        copy = remote(ref, ref, send_sem, recv_sem, moved(pos, axis, step))
        copy.start()
        sent.append(copy)

    def arrived(ref, recv_sem):
        remote(ref, ref, recv_sem, recv_sem, moved(pos, "c", 1)).wait_recv()

    offs = (0, -1, 1, 2)

    def onward(j):
        ref = unit(offs[j], 0, every)
        send(ref, bsend.at[f, j, 0], brecv.at[f, j, 0], B, 1)
        send(ref, bsend.at[f, j, 1], brecv.at[f, j, 1], B, -1)
        across(j, 0)

    def across(j, k):
        send(unit(offs[j], offs[k], every), csend.at[f, j, k], crecv.at[f, j, k], "c", 1)

    ref = unit(0, 0, every)
    send(ref, asend.at[f, 0], arecv.at[f, 0], A, 1)
    send(ref, asend.at[f, 1], arecv.at[f, 1], A, -1)
    onward(0)
    yield
    arrived(unit(-1, 0, every), arecv.at[f, 0])
    send(unit(-1, 0, low), asend.at[f, 2], arecv.at[f, 2], A, 1)
    onward(1)
    arrived(unit(1, 0, every), arecv.at[f, 1])
    send(unit(1, 0, high), asend.at[f, 3], arecv.at[f, 3], A, -1)
    onward(2)
    yield

    def relay(j):
        arrived(unit(offs[j], -1, every), brecv.at[f, j, 0])
        send(unit(offs[j], -1, low), bsend.at[f, j, 2], brecv.at[f, j, 2], B, 1)
        across(j, 1)
        arrived(unit(offs[j], 1, every), brecv.at[f, j, 1])
        send(unit(offs[j], 1, high), bsend.at[f, j, 3], brecv.at[f, j, 3], B, -1)
        across(j, 2)

    relay(0)
    yield
    arrived(unit(2, 0, low), arecv.at[f, 2])
    arrived(unit(2, 0, high), arecv.at[f, 3])
    onward(3)
    yield
    relay(1)
    relay(2)
    yield
    relay(3)
    yield
    for j in range(4):
        arrived(unit(offs[j], 2, low), brecv.at[f, j, 2])
        arrived(unit(offs[j], 2, high), brecv.at[f, j, 3])
        across(j, 3)
    yield
    for j in range(4):
        for k in range(4):
            at = {A: lax.rem(a + offs[j] + N, N), B: lax.rem(b + offs[k] + N, N)}
            arrived(full.at[at["x"], at["z"], 1 - c, :, every], crecv.at[f, j, k])
    for copy in sent:
        copy.wait_send()


def run_all(gens):
    gens = list(gens)
    while gens:
        for g in list(gens):
            try:
                next(g)
            except StopIteration:
                gens.remove(g)


def plane_line(pos):
    x, z, y, c = (pos[a] for a in AXES)
    plane = [{"z": lax.rem(z + dz, N), "y": lax.rem(y + dy, N)} for dz in range(N) for dy in range(N) if dz or dy]
    line = [{"x": lax.rem(x + dx, N), "c": lax.rem(c + dc, 2)} for dx in range(N) for dc in range(2) if dx or dc]
    return plane, line


SCATTER = (
    (0, 768, ("x", "y"), "z"), (768, 768, ("z", "y"), "x"), (1536, 768, ("x", "z"), "y"),
    (2304, 1024, ("x", "y"), "z"), (3328, 1024, ("z", "y"), "x"), (4352, 768, ("x", "z"), "y"),
)
NS = len(SCATTER)
W = 1024
WY = 768
TILE = 256
PIECE = 512
OFF = (0, 1, 4, 7)
FILL = {6: 2, 7: 2, 8: 2, 9: 2, 10: 2}


def scatter_chunk(pos, f, gl, w, part, cs, cr, bs, br, bsy, bry, keep, ps, pr, out, csem, bsem, psend, precv):
    start, width, (A, A2), B = SCATTER[f]
    a, a2, b, c, y = pos[A], pos[A2], pos[B], pos["c"], pos["y"]
    f32, bf16 = jnp.float32, jnp.bfloat16
    part = part.at[f, :, :, :width]
    cs, cr = cs.at[f, :, :, :width], cr.at[f, :, :, :width]
    bs, br = bs.at[f, :, :, :, :width], br.at[f, :, :, :, :width]
    bsy, bry = bsy.at[f // 3], bry.at[f // 3]
    keep, ps, pr = keep.at[f, :, :, :width], ps.at[f, :, :, :, :width], pr.at[f, :, :, :width]
    sent = []

    def index(ia, ib):
        at = {A: ia, B: ib}
        return at["x"] * N + at["z"]

    def shift(p, s):
        return lax.rem(p + s, N)

    def send(src, dst, ssem, rsem, device):
        copy = remote(src, dst, ssem, rsem, device)
        copy.start()
        sent.append(copy)

    def arrived(ref, rsem):
        remote(ref, ref, rsem, rsem, moved(pos, "c", 1)).wait_recv()

    def product(i, carry):
        rows = w[pl.ds(pl.multiple_of(start + i * TILE, TILE), TILE), :]
        got = lax.dot_general(
            gl[...].reshape(512, 1024), rows, (((1,), (1,)), ((), ())), preferred_element_type=f32
        )
        some = pl.ds(pl.multiple_of(i * TILE, TILE), TILE)
        cs[:, :, some] = got[:256].reshape(16, 16, TILE).astype(bf16)
        part[:, :, some] = got[256:].reshape(16, 16, TILE)
        return carry

    lax.fori_loop(0, width // TILE, product, 0)
    send(cs, cr, csem.at[0, f], csem.at[1, f], moved(pos, "c", 1))
    yield
    arrived(cr, csem.at[1, f])

    def chip(u):
        return part[u] + cr[u].astype(f32)

    def offer(da, d2, ref):
        device = {A: shift(a, da), A2: shift(a2, d2)}
        send(ref, pr.at[a * N + a2], psend.at[f], precv.at[f], device)

    if B == "y":
        def rows_of(u, carry):
            v = chip(u)
            for k in range(N):
                bsy[k, u] = v[4 * k : 4 * k + 4, :].astype(bf16)
            return carry

        lax.fori_loop(0, 16, rows_of, 0)
        for d in (2, 1, 3):
            send(bsy.at[shift(y, d)], bry.at[d - 1], bsem.at[0, f, d - 1], bsem.at[1, f, d - 1], moved(pos, "y", d))
        yield
        for d in (1, 2, 3):
            arrived(bry.at[d - 1], bsem.at[1, f, d - 1])

        def line_sum(u):
            v = bsy[y, u].astype(f32) + bry[0, u].astype(f32)
            return v + bry[1, u].astype(f32) + bry[2, u].astype(f32)

        for da in (2, 1, 3, 0):
            for d2 in (2, 1, 3, 0):
                v = line_sum(shift(a, da) * N + shift(a2, d2))
                if da or d2:
                    ps[da, d2] = v.astype(bf16)
                    offer(da, d2, ps.at[da, d2])
                else:
                    keep[0] = v
    else:
        for d in (2, 1, 3):
            def sums(i, carry):
                bs[d - 1, i] = chip(index(i, shift(b, d))).astype(bf16)
                return carry

            lax.fori_loop(0, N, sums, 0)
            send(bs.at[d - 1], br.at[d - 1], bsem.at[0, f, d - 1], bsem.at[1, f, d - 1], moved(pos, B, d))
        yield
        for d in (1, 2, 3):
            arrived(br.at[d - 1], bsem.at[1, f, d - 1])
        for da in (2, 1, 3, 0):
            to = shift(a, da)
            v = chip(index(to, b)) + br[0, to].astype(f32) + br[1, to].astype(f32) + br[2, to].astype(f32)
            for k in range(N):
                ps[da, k] = v[4 * k : 4 * k + 4, :].astype(bf16)
                if da == 0:
                    keep[k] = v[4 * k : 4 * k + 4, :]
            for d2 in (2, 1, 3, 0):
                if da or d2:
                    offer(da, d2, ps.at[da, shift(y, d2)])
    yield
    group = pr.at[pl.ds(0, 15)]
    arrived(group, precv.at[f])
    mine = a * N + a2
    total = keep[0] if B == "y" else keep[y]
    for d in range(1, 16):
        total = total + pr[lax.rem(mine + d, 16)].astype(f32)
    out[:, start : start + width] = total.astype(bf16)
    for copy in sent:
        copy.wait_send()


def step_kernel(h, tl, bl, rr, tail_in, weight_in, w_hbm, loss, gx, gh,
                tout, tmap, tcon, extra, CH, full, inc, rows, wide, w, L, gl, far_gl, T32, TV, msg, near, mid, far, lmsg, lnear, lmid, lfar,
                part, cs, cr, bs, br, bsy, bry, kept_rows, ps, pr, stage,
                wsem, ysend, yrecv, asend, arecv, bsend, brecv, csend, crecv, tsend, trecv, own, zsem, every, pair,
                xsem, rcsem, rbsem, psend, precv, gsem):
    f32, bf16 = jnp.float32, jnp.bfloat16
    pos = spot()
    x, z, y, c = (pos[a] for a in AXES)
    me = ((x * N + z) * N + y) * 2 + c
    plane, line = plane_line(pos)
    loads = []
    for f, (start, width, _, _) in enumerate(CHUNKS):
        copy = pltpu.make_async_copy(w_hbm.at[pl.ds(start, width)], w.at[pl.ds(start, width)], wsem.at[f])
        copy.start()
        loads.append(copy)
    greet(pos, lines(pos, AXES))

    first = []
    for f, (start, width, _, _) in enumerate(CHUNKS):
        cols = pl.ds(start, width)
        for d in (2, 1, 3):
            copy = remote(
                h.at[:, cols], rows.at[y, :, cols], ysend.at[f, d - 1], yrecv.at[f, d - 1], moved(pos, "y", d)
            )
            copy.start()
            first.append(copy)
    for device in lines(pos, ("z",)):
        pl.semaphore_signal(zsem, inc=1, device_id=device, device_id_type=pl.DeviceIdType.MESH)
    rows[y] = h[...]

    def iota(shape, axis):
        return lax.broadcasted_iota(jnp.int32, shape, axis)

    stored = rr[...]
    place = (((stored >> 5) * 2 + ((stored >> 2) & 1)) * 4 + ((stored >> 3) & 3)) * 4 + (stored & 3)
    lane = iota((4, 128), 1)
    mine = jnp.sum(jnp.where(lane == me, place.astype(f32), 0.0), axis=1, keepdims=True)
    here = lane.astype(f32) == mine

    def norms(t):
        v = tl[t].astype(f32)
        top = jnp.max(jnp.max(v, axis=0, keepdims=True), axis=1, keepdims=True)
        total = jnp.sum(jnp.sum(jnp.exp(v - top), axis=0, keepdims=True), axis=1, keepdims=True)
        tcon[t : t + 1] = jnp.where(here[t : t + 1], top + jnp.log(total), -1e30)
        at = jnp.broadcast_to(place[t : t + 1], (128, 128))
        tmap[t] = jnp.where(iota((128, 128), 0) == at, 1.0, 0.0).astype(bf16)

    def slots(t):
        lists = bl[t : t + 1]
        owner = lists >> 3
        held = jnp.where(iota((128, 256), 0) == owner, 1.0, 0.0)
        before = jnp.where(iota((256, 256), 0) < iota((256, 256), 1), 1.0, 0.0).astype(bf16)
        seen = jnp.dot(held.astype(bf16), before, preferred_element_type=f32)
        rank = jnp.sum(held * seen, axis=0, keepdims=True).astype(jnp.int32)
        pick = jnp.where(iota((512, 256), 0) == rank * 128 + owner, 1.0, 0.0).astype(bf16)
        got = jnp.dot(pick, tl[t], preferred_element_type=f32)
        for m in range(MOST):
            T32[pl.ds(t * MOST + m, 128, stride=16), :] = got[128 * m : 128 * m + 128]
        local = jnp.where(owner == me, rank * 8 + (lists & 7), -1)
        kept = jnp.sum(jnp.where(iota((32, 256), 0) == local, 1.0, 0.0), axis=1, keepdims=True)
        CH[t] = jnp.broadcast_to(kept, (32, 128))

    norms(0)
    norms(1)
    gens = []
    for f, (start, width, _, _) in enumerate(CHUNKS):
        cols = pl.ds(start, width)
        for d in (1, 2, 3):
            ref = rows.at[lax.rem(y - d + N, N), :, cols]
            remote(ref, ref, ysend.at[f, d - 1], yrecv.at[f, d - 1], moved(pos, "y", d)).wait_recv()
        for k in range(N):
            wide[4 * k : 4 * k + 4, cols] = rows[k, :, cols].astype(f32)
        full[x, z, c, :, cols] = wide[:, cols].astype(bf16)
        g = gather_chunk(pos, f, full, asend, arecv, bsend, brecv, csend, crecv)
        next(g)
        gens.append(g)
    slots(0)
    slots(1)
    pl.semaphore_wait(zsem, 3)
    for device in lines(pos, ("x",)):
        pl.semaphore_signal(every, inc=1, device_id=device, device_id_type=pl.DeviceIdType.MESH)

    def one(k, carry):
        to = lax.rem(me + k, 128)
        device = {"x": to // 32, "z": lax.rem(to // 8, N), "y": lax.rem(to // 2, N), "c": lax.rem(to, 2)}
        remote(tout.at[to], inc.at[me], tsend, trecv, device).start()
        return carry

    def logits_part(f, lo, hi):
        start, width = CHUNKS[f][:2]

        def tile(i, carry):
            cols = pl.ds(pl.multiple_of(i * TILE, TILE), TILE)
            got = jnp.dot(
                full[:, :, :, :, start : start + width].reshape(512, width),
                w[start : start + width, cols],
                preferred_element_type=f32,
            )
            if f == 0:
                L[:, cols] = got
            else:
                L[:, cols] += got
            return carry

        lax.fori_loop(lo, hi, tile, 0)

    def finish(g):
        for _ in g:
            pass

    g0, g1, g2, g3 = gens
    next(g0), next(g1)
    next(g2), next(g3)
    slots(2)
    next(g0), next(g1)
    slots(3)
    next(g2), next(g3)
    norms(2)
    norms(3)
    pl.semaphore_wait(every, 3)
    pl.semaphore_signal(pair, inc=1, device_id=moved(pos, "c", 1), device_id_type=pl.DeviceIdType.MESH)
    next(g0), next(g1)
    tout[...] = T32[...].reshape(128, 16, 128).astype(bf16)
    keep = pltpu.make_async_copy(tout.at[me], inc.at[me], own.at[0])
    keep.start()
    pl.semaphore_wait(pair, 1)
    next(g2), next(g3)
    next(g0), next(g1)
    natural = iota((128, 128), 1)
    natural = (natural >> 5) * 32 + ((natural >> 2) & 3) * 8 + ((natural >> 4) & 1) * 4 + (natural & 3)
    turn = jnp.where(iota((128, 128), 0) == natural, 1.0, 0.0)
    extra[0:4] = tail_in[...]
    extra[4:8] = weight_in[...]
    extra[...] = jnp.dot(extra[...], turn, preferred_element_type=f32, precision=lax.Precision.HIGHEST)
    next(g2), next(g3)
    next(g0), next(g1)
    finish(g0)
    next(g2), next(g3)
    loads[0].wait()
    logits_part(0, 0, 2)
    next(g2), next(g3)
    lax.fori_loop(1, 128, one, 0)
    logits_part(0, 2, 4)
    finish(g1)
    loads[1].wait()
    logits_part(1, 0, 4)
    finish(g2)
    loads[2].wait()
    logits_part(2, 0, 4)
    finish(g3)
    loads[3].wait()
    logits_part(3, 0, 4)
    for copy in first:
        copy.wait_send()

    for t in range(N):
        r = slice(128 * t, 128 * t + 128)
        top = L[r, :128]
        for b in range(1, 8):
            top = jnp.maximum(top, L[r, 128 * b : 128 * b + 128])
        col = jnp.max(top, axis=1, keepdims=True)
        acc = jnp.exp(L[r, :128] - col)
        for b in range(1, 8):
            acc = acc + jnp.exp(L[r, 128 * b : 128 * b + 128] - col)
        msg[0, t : t + 1] = jnp.max(top.T, axis=0, keepdims=True)
        msg[1, t : t + 1] = jnp.sum(acc.T, axis=0, keepdims=True)
    msg[0, 4:8] = tcon[0:4]
    msg[1, 4:8] = jnp.zeros((4, 128), f32)

    def merge(parts):
        top = parts[0][0]
        for p in parts[1:]:
            top = jnp.maximum(top, p[0])
        total = 0.0
        for p in parts:
            total += p[1] * jnp.exp(p[0] - top)
        return top, total

    for device in plane:
        remote(msg, near.at[z * N + y], xsem.at[0], xsem.at[1], device).start()
    near[z * N + y] = msg[...]

    part_inc = inc.at[pl.ds(0, 127)]
    remote(part_inc, part_inc, tsend, trecv, moved(pos, "c", 1)).wait()
    keep.wait()
    T32[...] = inc[...].reshape(2048, 128).astype(f32)

    def teacher(t):
        stored = jnp.concatenate(
            [T32[pl.ds(t * MOST + m, 128, stride=16), :] for m in range(MOST)], axis=1
        ).astype(bf16)
        ordered = jnp.dot(tmap[t], stored, preferred_element_type=f32)
        for b in range(8):
            v = CH[t, b : b + 1] * ordered[:, :128]
            for m in range(1, MOST):
                v = v + CH[t, m * 8 + b : m * 8 + b + 1] * ordered[:, 128 * m : 128 * m + 128]
            TV[t, b] = v.astype(bf16)

    teacher(0)
    teacher(1)
    group = near.at[pl.ds(0, 15)]
    remote(group, group, xsem.at[0], xsem.at[1], plane[0]).wait()
    mid[0], mid[1] = merge([near[i] for i in range(16)])
    for device in line:
        remote(mid, far.at[x * 2 + c], xsem.at[2], xsem.at[3], device).start()
    far[x * 2 + c] = mid[...]
    teacher(2)
    teacher(3)
    group = far.at[pl.ds(0, 7)]
    remote(group, group, xsem.at[2], xsem.at[3], line[0]).wait()
    top, total = merge([far[i] for i in range(8)])

    log_norm = top[0:4] + jnp.log(total[0:4])
    tail = extra[0:4]
    weight = extra[4:8]
    kept = jnp.log(1.0 - tail) - top[4:8]
    tail_prob = tail / UNLISTED
    tail_log = jnp.log(tail_prob)

    def column(v, t):
        return jnp.broadcast_to(v[t : t + 1], (128, 128)).T

    lmsg[...] = jnp.zeros((8, 128), f32)
    for t in range(N):
        r = slice(128 * t, 128 * t + 128)
        norm_c, weight_c, kept_c = column(log_norm, t), column(weight, t), column(kept, t)
        prob_c, log_c = column(tail_prob, t), column(tail_log, t)
        acc = jnp.zeros((128, 128), f32)
        for b in range(8):
            scores = L[r, 128 * b : 128 * b + 128]
            on = CH[t, b : b + 1] + CH[t, 8 + b : 9 + b] + CH[t, 16 + b : 17 + b] + CH[t, 24 + b : 25 + b]
            off = 1.0 - on
            listed_log = TV[t, b].astype(f32) + kept_c
            q = on * jnp.exp(listed_log) + off * prob_c
            log_q = on * listed_log + off * log_c
            gap = scores - norm_c
            g = (weight_c * (jnp.exp(gap) - q)).astype(bf16)
            gl[r, 128 * b : 128 * b + 128] = g
            g = g.reshape(4, 2, 16, 128)
            far_gl[c, 4 * t : 4 * t + 4, :, 128 * b : 128 * b + 128] = g[:, 1]
            far_gl[1 - c, 4 * t : 4 * t + 4, :, 128 * b : 128 * b + 128] = g[:, 0]
            acc = acc + q * (log_q - gap)
        lmsg[t : t + 1] = jnp.sum(acc.T, axis=0, keepdims=True)

    stores = [None, None]
    count = [0]

    def head_pieces(n):
        lo = count[0]
        count[0] = lo + n

        def piece(i, carry):
            some = pl.ds(pl.multiple_of(i * PIECE, PIECE), PIECE)
            gh[some, :] = lax.dot_general(
                full[:, :, :, :, some].reshape(512, PIECE), gl[...], (((0,), (0,)), ((), ())),
                preferred_element_type=f32,
            ).astype(bf16)
            return carry

        lax.fori_loop(lo, lo + n, piece, 0)

    chunks = [
        scatter_chunk(pos, f, far_gl, w, part, cs, cr, bs, br, bsy, bry, kept_rows, ps, pr, gx, rcsem, rbsem, psend, precv)
        for f in range(NS)
    ]
    for tick in range(NS + OFF[-1]):
        for f in reversed(range(NS)):
            if tick - f in OFF:
                next(chunks[f], None)
        if tick == 0:
            for device in plane:
                remote(lmsg, lnear.at[z * N + y], xsem.at[4], xsem.at[5], device).start()
            lnear[z * N + y] = lmsg[...]
        if tick == OFF[1] + 3:
            group = lnear.at[pl.ds(0, 15)]
            remote(group, group, xsem.at[4], xsem.at[5], plane[0]).wait()
            total = lnear[0]
            for i in range(1, 16):
                total = total + lnear[i]
            lmid[...] = total
            for device in line:
                remote(lmid, lfar.at[x * 2 + c], xsem.at[6], xsem.at[7], device).start()
            lfar[x * 2 + c] = lmid[...]
        if tick in FILL:
            head_pieces(FILL[tick])
    group = lfar.at[pl.ds(0, 7)]
    remote(group, group, xsem.at[6], xsem.at[7], line[0]).wait()
    total = lfar[0]
    for i in range(1, 8):
        total = total + lfar[i]
    row = jnp.sum(jnp.where(iota((8, 128), 0) == x, total, 0.0), axis=0, keepdims=True)
    lanes = iota((128, 128), 1)
    pick = jnp.where((iota((128, 128), 0) == (z * 2 + c) * 16 + y * 4 + lanes) & (lanes < 4), 1.0, 0.0)
    loss[...] = jnp.dot(
        jnp.broadcast_to(row, (8, 128)), pick, preferred_element_type=f32, precision=lax.Precision.HIGHEST
    )


UNLISTED = 98304.0


def step(hidden, teacher, lists, reader, tail, weight, head):
    bf16, f32 = jnp.bfloat16, jnp.float32
    V = pltpu.VMEM
    return pl.pallas_call(
        step_kernel,
        out_shape=(
            jax.ShapeDtypeStruct((8, 128), f32),
            jax.ShapeDtypeStruct((4, D), bf16),
            pltpu.VMEM(head.shape, bf16),
        ),
        in_specs=[VM, VM, VM, VM, VM, VM, ANY],
        out_specs=(VM, VM, VM),
        scratch_shapes=[
            V((128, 16, 128), bf16), V((N, 128, 128), bf16), V((N, 128), f32), V((8, 128), f32), V((N, 32, 128), f32),
            V((N, N, 2, 16, D), bf16),
            V((128, 16, 128), bf16),
            V((N, 4, D), bf16),
            V((16, D), f32),
            V(head.shape, bf16),
            V((512, 1024), f32),
            V((512, 1024), bf16),
            V((2, 16, 16, 1024), bf16),
            V((2048, 128), f32),
            V((N, 8, 128, 128), bf16),
            V((2, 8, 128), f32), V((16, 2, 8, 128), f32), V((2, 8, 128), f32), V((8, 2, 8, 128), f32),
            V((8, 128), f32), V((16, 8, 128), f32), V((8, 128), f32), V((8, 8, 128), f32),
            V((NS, 16, 16, W), f32),
            V((NS, 16, 16, W), bf16), V((NS, 16, 16, W), bf16),
            V((NS, 3, N, 16, W), bf16), V((NS, 3, N, 16, W), bf16),
            V((2, N, 16, 4, WY), bf16), V((2, 3, 16, 4, WY), bf16),
            V((NS, N, 4, W), f32),
            V((NS, N, N, 4, W), bf16), V((NS, 16, 4, W), bf16),
            V((8, 128), bf16),
            DMA((NC,)),
            DMA((NC, 3)), DMA((NC, 3)),
            DMA((NC, 4)), DMA((NC, 4)),
            DMA((NC, 4, 4)), DMA((NC, 4, 4)),
            DMA((NC, 4, 4)), DMA((NC, 4, 4)),
            DMA, DMA, DMA((2,)), REGULAR, REGULAR, REGULAR,
            DMA((8,)),
            DMA((2, NS)), DMA((2, NS, 3)), DMA((NS,)), DMA((NS,)), DMA((2,)),
        ],
        compiler_params=pltpu.CompilerParams(collective_id=0, has_side_effects=True, vmem_limit_bytes=53 << 20),
        name="step",
    )(hidden, teacher, lists, reader, tail, weight, head)


def on_device(
    hidden_states, head_weight, teacher_logits, block_lists, row_reader, tail_mass, token_weight
):
    row_loss, grad_hidden, grad_head = step(
        hidden_states, teacher_logits[:, :, 0, :], block_lists, row_reader, tail_mass.reshape(N, 128), token_weight.reshape(N, 128), head_weight
    )
    token_loss = row_loss[0, :4]
    return (token_loss, grad_head, grad_hidden)


def solution(mesh):
    split = Mesh(mesh.devices.reshape(N, N, N, 2), AXES)
    return jax.shard_map(
        on_device,
        mesh=split,
        in_specs=(P(AXES, None), P(None, AXES), P(None, None, AXES, None), P(), P(), P(), P()),
        out_specs=(P(AXES), P(None, AXES), P(AXES, None)),
        check_vma=False,
    )
```

```python
import functools

import jax
import jax.numpy as jnp
from jax import lax
from jax.experimental import pallas as pl
from jax.experimental.pallas import tpu as pltpu
from jax.sharding import Mesh
from jax.sharding import PartitionSpec as P

MOST = 4
AXES = ("x", "z", "y", "c")
N = 4
D = 5120
CHUNKS = ((0, 1280, "x", "z"), (1280, 1280, "z", "x"), (2560, 1280, "x", "z"), (3840, 1280, "z", "x"))
NC = len(CHUNKS)
DMA = pltpu.SemaphoreType.DMA
REGULAR = pltpu.SemaphoreType.REGULAR
VM = pl.BlockSpec(memory_space=pltpu.VMEM)
ANY = pl.BlockSpec(memory_space=pl.ANY)


def spot():
    return {a: lax.axis_index(a) for a in AXES}


def moved(pos, axis, step):
    if axis == "c":
        return {"c": 1 - pos["c"]}
    return {axis: lax.rem(pos[axis] + step + N, N)}


def remote(src, dst, send, recv, device):
    return pltpu.make_async_remote_copy(
        src_ref=src, dst_ref=dst, send_sem=send, recv_sem=recv,
        device_id=device, device_id_type=pl.DeviceIdType.MESH,
    )


def greet(pos, partners):
    barrier = pltpu.get_barrier_semaphore()
    for device in partners:
        pl.semaphore_signal(barrier, inc=1, device_id=device, device_id_type=pl.DeviceIdType.MESH)
    pl.semaphore_wait(barrier, len(partners))


def lines(pos, axes):
    return [moved(pos, a, s) for a in axes for s in ((1,) if a == "c" else (1, 2, 3))]


def gather_chunk(pos, f, full, asend, arecv, bsend, brecv, csend, crecv):
    start, width, A, B = CHUNKS[f]
    half = width // 2
    a, b, c = pos[A], pos[B], pos["c"]
    every, low, high = pl.ds(start, width), pl.ds(start, half), pl.ds(start + half, half)
    sent = []

    def unit(off_a, off_b, cols):
        at = {A: lax.rem(a + off_a + N, N), B: lax.rem(b + off_b + N, N)}
        return full.at[at["x"], at["z"], c, :, cols]

    def send(ref, send_sem, recv_sem, axis, step):
        copy = remote(ref, ref, send_sem, recv_sem, moved(pos, axis, step))
        copy.start()
        sent.append(copy)

    def arrived(ref, recv_sem):
        remote(ref, ref, recv_sem, recv_sem, moved(pos, "c", 1)).wait_recv()

    offs = (0, -1, 1, 2)

    def onward(j):
        ref = unit(offs[j], 0, every)
        send(ref, bsend.at[f, j, 0], brecv.at[f, j, 0], B, 1)
        send(ref, bsend.at[f, j, 1], brecv.at[f, j, 1], B, -1)
        across(j, 0)

    def across(j, k):
        send(unit(offs[j], offs[k], every), csend.at[f, j, k], crecv.at[f, j, k], "c", 1)

    ref = unit(0, 0, every)
    send(ref, asend.at[f, 0], arecv.at[f, 0], A, 1)
    send(ref, asend.at[f, 1], arecv.at[f, 1], A, -1)
    onward(0)
    yield
    arrived(unit(-1, 0, every), arecv.at[f, 0])
    send(unit(-1, 0, low), asend.at[f, 2], arecv.at[f, 2], A, 1)
    onward(1)
    arrived(unit(1, 0, every), arecv.at[f, 1])
    send(unit(1, 0, high), asend.at[f, 3], arecv.at[f, 3], A, -1)
    onward(2)
    yield

    def relay(j):
        arrived(unit(offs[j], -1, every), brecv.at[f, j, 0])
        send(unit(offs[j], -1, low), bsend.at[f, j, 2], brecv.at[f, j, 2], B, 1)
        across(j, 1)
        arrived(unit(offs[j], 1, every), brecv.at[f, j, 1])
        send(unit(offs[j], 1, high), bsend.at[f, j, 3], brecv.at[f, j, 3], B, -1)
        across(j, 2)

    relay(0)
    yield
    arrived(unit(2, 0, low), arecv.at[f, 2])
    arrived(unit(2, 0, high), arecv.at[f, 3])
    onward(3)
    yield
    relay(1)
    relay(2)
    yield
    relay(3)
    yield
    for j in range(4):
        arrived(unit(offs[j], 2, low), brecv.at[f, j, 2])
        arrived(unit(offs[j], 2, high), brecv.at[f, j, 3])
        across(j, 3)
    yield
    for j in range(4):
        for k in range(4):
            at = {A: lax.rem(a + offs[j] + N, N), B: lax.rem(b + offs[k] + N, N)}
            arrived(full.at[at["x"], at["z"], 1 - c, :, every], crecv.at[f, j, k])
    for copy in sent:
        copy.wait_send()


def run_all(gens):
    gens = list(gens)
    while gens:
        for g in list(gens):
            try:
                next(g)
            except StopIteration:
                gens.remove(g)


def plane_line(pos):
    x, z, y, c = (pos[a] for a in AXES)
    plane = [{"z": lax.rem(z + dz, N), "y": lax.rem(y + dy, N)} for dz in range(N) for dy in range(N) if dz or dy]
    line = [{"x": lax.rem(x + dx, N), "c": lax.rem(c + dc, 2)} for dx in range(N) for dc in range(2) if dx or dc]
    return plane, line


SCATTER = (
    (0, 768, ("x", "y"), "z"), (768, 768, ("z", "y"), "x"), (1536, 768, ("x", "z"), "y"),
    (2304, 1024, ("x", "y"), "z"), (3328, 1024, ("z", "y"), "x"), (4352, 768, ("x", "z"), "y"),
)
NS = len(SCATTER)
W = 1024
WY = 768
TILE = 256
PIECE = 512
OFF = (0, 1, 4, 7)
FILL = {6: 2, 7: 2, 8: 2, 9: 2, 10: 2}


def scatter_chunk(pos, f, gl, w, part, cs, cr, bs, br, bsy, bry, keep, ps, pr, out, csem, bsem, psend, precv):
    start, width, (A, A2), B = SCATTER[f]
    a, a2, b, c, y = pos[A], pos[A2], pos[B], pos["c"], pos["y"]
    f32, bf16 = jnp.float32, jnp.bfloat16
    part = part.at[f, :, :, :width]
    cs, cr = cs.at[f, :, :, :width], cr.at[f, :, :, :width]
    bs, br = bs.at[f, :, :, :, :width], br.at[f, :, :, :, :width]
    bsy, bry = bsy.at[f // 3], bry.at[f // 3]
    keep, ps, pr = keep.at[f, :, :, :width], ps.at[f, :, :, :, :width], pr.at[f, :, :, :width]
    sent = []

    def index(ia, ib):
        at = {A: ia, B: ib}
        return at["x"] * N + at["z"]

    def shift(p, s):
        return lax.rem(p + s, N)

    def send(src, dst, ssem, rsem, device):
        copy = remote(src, dst, ssem, rsem, device)
        copy.start()
        sent.append(copy)

    def arrived(ref, rsem):
        remote(ref, ref, rsem, rsem, moved(pos, "c", 1)).wait_recv()

    def product(i, carry):
        rows = w[pl.ds(pl.multiple_of(start + i * TILE, TILE), TILE), :]
        got = lax.dot_general(
            gl[...].reshape(512, 1024), rows, (((1,), (1,)), ((), ())), preferred_element_type=f32
        )
        some = pl.ds(pl.multiple_of(i * TILE, TILE), TILE)
        cs[:, :, some] = got[:256].reshape(16, 16, TILE).astype(bf16)
        part[:, :, some] = got[256:].reshape(16, 16, TILE)
        return carry

    lax.fori_loop(0, width // TILE, product, 0)
    send(cs, cr, csem.at[0, f], csem.at[1, f], moved(pos, "c", 1))
    yield
    arrived(cr, csem.at[1, f])

    def chip(u):
        return part[u] + cr[u].astype(f32)

    def offer(da, d2, ref):
        device = {A: shift(a, da), A2: shift(a2, d2)}
        send(ref, pr.at[a * N + a2], psend.at[f], precv.at[f], device)

    if B == "y":
        def rows_of(u, carry):
            v = chip(u)
            for k in range(N):
                bsy[k, u] = v[4 * k : 4 * k + 4, :].astype(bf16)
            return carry

        lax.fori_loop(0, 16, rows_of, 0)
        for d in (2, 1, 3):
            send(bsy.at[shift(y, d)], bry.at[d - 1], bsem.at[0, f, d - 1], bsem.at[1, f, d - 1], moved(pos, "y", d))
        yield
        for d in (1, 2, 3):
            arrived(bry.at[d - 1], bsem.at[1, f, d - 1])

        def line_sum(u):
            v = bsy[y, u].astype(f32) + bry[0, u].astype(f32)
            return v + bry[1, u].astype(f32) + bry[2, u].astype(f32)

        for da in (2, 1, 3, 0):
            for d2 in (2, 1, 3, 0):
                v = line_sum(shift(a, da) * N + shift(a2, d2))
                if da or d2:
                    ps[da, d2] = v.astype(bf16)
                    offer(da, d2, ps.at[da, d2])
                else:
                    keep[0] = v
    else:
        for d in (2, 1, 3):
            def sums(i, carry):
                bs[d - 1, i] = chip(index(i, shift(b, d))).astype(bf16)
                return carry

            lax.fori_loop(0, N, sums, 0)
            send(bs.at[d - 1], br.at[d - 1], bsem.at[0, f, d - 1], bsem.at[1, f, d - 1], moved(pos, B, d))
        yield
        for d in (1, 2, 3):
            arrived(br.at[d - 1], bsem.at[1, f, d - 1])
        for da in (2, 1, 3, 0):
            to = shift(a, da)
            v = chip(index(to, b)) + br[0, to].astype(f32) + br[1, to].astype(f32) + br[2, to].astype(f32)
            for k in range(N):
                ps[da, k] = v[4 * k : 4 * k + 4, :].astype(bf16)
                if da == 0:
                    keep[k] = v[4 * k : 4 * k + 4, :]
            for d2 in (2, 1, 3, 0):
                if da or d2:
                    offer(da, d2, ps.at[da, shift(y, d2)])
    yield
    group = pr.at[pl.ds(0, 15)]
    arrived(group, precv.at[f])
    mine = a * N + a2
    total = keep[0] if B == "y" else keep[y]
    for d in range(1, 16):
        total = total + pr[lax.rem(mine + d, 16)].astype(f32)
    out[:, start : start + width] = total.astype(bf16)
    for copy in sent:
        copy.wait_send()


def step_kernel(h, tl, bl, rr, tail_in, weight_in, w_hbm, loss, gx, gh,
                tout, tmap, tcon, extra, CH, full, inc, rows, wide, w, L, gl, far_gl, T32, TV, msg, near, mid, far, lmsg, lnear, lmid, lfar,
                part, cs, cr, bs, br, bsy, bry, kept_rows, ps, pr, stage,
                wsem, ysend, yrecv, asend, arecv, bsend, brecv, csend, crecv, tsend, trecv, own, zsem, every, pair,
                xsem, rcsem, rbsem, psend, precv, gsem):
    f32, bf16 = jnp.float32, jnp.bfloat16
    pos = spot()
    x, z, y, c = (pos[a] for a in AXES)
    me = ((x * N + z) * N + y) * 2 + c
    plane, line = plane_line(pos)
    loads = []
    for f, (start, width, _, _) in enumerate(CHUNKS):
        copy = pltpu.make_async_copy(w_hbm.at[pl.ds(start, width)], w.at[pl.ds(start, width)], wsem.at[f])
        copy.start()
        loads.append(copy)
    greet(pos, lines(pos, AXES))

    first = []
    for f, (start, width, _, _) in enumerate(CHUNKS):
        cols = pl.ds(start, width)
        for d in (2, 1, 3):
            copy = remote(
                h.at[:, cols], rows.at[y, :, cols], ysend.at[f, d - 1], yrecv.at[f, d - 1], moved(pos, "y", d)
            )
            copy.start()
            first.append(copy)
    for device in lines(pos, ("z",)):
        pl.semaphore_signal(zsem, inc=1, device_id=device, device_id_type=pl.DeviceIdType.MESH)
    rows[y] = h[...]

    def iota(shape, axis):
        return lax.broadcasted_iota(jnp.int32, shape, axis)

    stored = rr[...]
    place = (((stored >> 5) * 2 + ((stored >> 2) & 1)) * 4 + ((stored >> 3) & 3)) * 4 + (stored & 3)
    lane = iota((4, 128), 1)
    mine = jnp.sum(jnp.where(lane == me, place.astype(f32), 0.0), axis=1, keepdims=True)
    here = lane.astype(f32) == mine

    def norms(t):
        v = tl[t].astype(f32)
        top = jnp.max(jnp.max(v, axis=0, keepdims=True), axis=1, keepdims=True)
        total = jnp.sum(jnp.sum(jnp.exp(v - top), axis=0, keepdims=True), axis=1, keepdims=True)
        tcon[t : t + 1] = jnp.where(here[t : t + 1], top + jnp.log(total), -1e30)
        at = jnp.broadcast_to(place[t : t + 1], (128, 128))
        tmap[t] = jnp.where(iota((128, 128), 0) == at, 1.0, 0.0).astype(bf16)

    def slots(t):
        lists = bl[t : t + 1]
        owner = lists >> 3
        held = jnp.where(iota((128, 256), 0) == owner, 1.0, 0.0)
        before = jnp.where(iota((256, 256), 0) < iota((256, 256), 1), 1.0, 0.0).astype(bf16)
        seen = jnp.dot(held.astype(bf16), before, preferred_element_type=f32)
        rank = jnp.sum(held * seen, axis=0, keepdims=True).astype(jnp.int32)
        pick = jnp.where(iota((512, 256), 0) == rank * 128 + owner, 1.0, 0.0).astype(bf16)
        got = jnp.dot(pick, tl[t], preferred_element_type=f32)
        for m in range(MOST):
            T32[pl.ds(t * MOST + m, 128, stride=16), :] = got[128 * m : 128 * m + 128]
        local = jnp.where(owner == me, rank * 8 + (lists & 7), -1)
        kept = jnp.sum(jnp.where(iota((32, 256), 0) == local, 1.0, 0.0), axis=1, keepdims=True)
        CH[t] = jnp.broadcast_to(kept, (32, 128))

    norms(0)
    norms(1)
    gens = []
    for f, (start, width, _, _) in enumerate(CHUNKS):
        cols = pl.ds(start, width)
        for d in (1, 2, 3):
            ref = rows.at[lax.rem(y - d + N, N), :, cols]
            remote(ref, ref, ysend.at[f, d - 1], yrecv.at[f, d - 1], moved(pos, "y", d)).wait_recv()
        for k in range(N):
            wide[4 * k : 4 * k + 4, cols] = rows[k, :, cols].astype(f32)
        full[x, z, c, :, cols] = wide[:, cols].astype(bf16)
        g = gather_chunk(pos, f, full, asend, arecv, bsend, brecv, csend, crecv)
        next(g)
        gens.append(g)
    slots(0)
    slots(1)
    pl.semaphore_wait(zsem, 3)
    for device in lines(pos, ("x",)):
        pl.semaphore_signal(every, inc=1, device_id=device, device_id_type=pl.DeviceIdType.MESH)

    def one(k, carry):
        to = lax.rem(me + k, 128)
        device = {"x": to // 32, "z": lax.rem(to // 8, N), "y": lax.rem(to // 2, N), "c": lax.rem(to, 2)}
        remote(tout.at[to], inc.at[me], tsend, trecv, device).start()
        return carry

    def logits_part(f, lo, hi):
        start, width = CHUNKS[f][:2]

        def tile(i, carry):
            cols = pl.ds(pl.multiple_of(i * TILE, TILE), TILE)
            got = jnp.dot(
                full[:, :, :, :, start : start + width].reshape(512, width),
                w[start : start + width, cols],
                preferred_element_type=f32,
            )
            if f == 0:
                L[:, cols] = got
            else:
                L[:, cols] += got
            return carry

        lax.fori_loop(lo, hi, tile, 0)

    def finish(g):
        for _ in g:
            pass

    g0, g1, g2, g3 = gens
    next(g0), next(g1)
    next(g2), next(g3)
    slots(2)
    next(g0), next(g1)
    slots(3)
    next(g2), next(g3)
    norms(2)
    norms(3)
    pl.semaphore_wait(every, 3)
    pl.semaphore_signal(pair, inc=1, device_id=moved(pos, "c", 1), device_id_type=pl.DeviceIdType.MESH)
    next(g0), next(g1)
    tout[...] = T32[...].reshape(128, 16, 128).astype(bf16)
    keep = pltpu.make_async_copy(tout.at[me], inc.at[me], own.at[0])
    keep.start()
    pl.semaphore_wait(pair, 1)
    next(g2), next(g3)
    next(g0), next(g1)
    natural = iota((128, 128), 1)
    natural = (natural >> 5) * 32 + ((natural >> 2) & 3) * 8 + ((natural >> 4) & 1) * 4 + (natural & 3)
    turn = jnp.where(iota((128, 128), 0) == natural, 1.0, 0.0)
    extra[0:4] = tail_in[...]
    extra[4:8] = weight_in[...]
    extra[...] = jnp.dot(extra[...], turn, preferred_element_type=f32, precision=lax.Precision.HIGHEST)
    next(g2), next(g3)
    next(g0), next(g1)
    next(g2), next(g3)
    finish(g0)
    next(g2), next(g3)
    lax.fori_loop(1, 128, one, 0)
    loads[0].wait()
    logits_part(0, 0, 4)
    finish(g1)
    loads[1].wait()
    logits_part(1, 0, 4)
    finish(g2)
    loads[2].wait()
    logits_part(2, 0, 4)
    finish(g3)
    loads[3].wait()
    logits_part(3, 0, 4)
    for copy in first:
        copy.wait_send()

    for t in range(N):
        r = slice(128 * t, 128 * t + 128)
        top = L[r, :128]
        for b in range(1, 8):
            top = jnp.maximum(top, L[r, 128 * b : 128 * b + 128])
        col = jnp.max(top, axis=1, keepdims=True)
        acc = jnp.exp(L[r, :128] - col)
        for b in range(1, 8):
            acc = acc + jnp.exp(L[r, 128 * b : 128 * b + 128] - col)
        msg[0, t : t + 1] = jnp.max(top.T, axis=0, keepdims=True)
        msg[1, t : t + 1] = jnp.sum(acc.T, axis=0, keepdims=True)
    msg[0, 4:8] = tcon[0:4]
    msg[1, 4:8] = jnp.zeros((4, 128), f32)

    def merge(parts):
        top = parts[0][0]
        for p in parts[1:]:
            top = jnp.maximum(top, p[0])
        total = 0.0
        for p in parts:
            total += p[1] * jnp.exp(p[0] - top)
        return top, total

    for device in plane:
        remote(msg, near.at[z * N + y], xsem.at[0], xsem.at[1], device).start()
    near[z * N + y] = msg[...]

    part_inc = inc.at[pl.ds(0, 127)]
    remote(part_inc, part_inc, tsend, trecv, moved(pos, "c", 1)).wait()
    keep.wait()
    T32[...] = inc[...].reshape(2048, 128).astype(f32)

    def teacher(t):
        stored = jnp.concatenate(
            [T32[pl.ds(t * MOST + m, 128, stride=16), :] for m in range(MOST)], axis=1
        ).astype(bf16)
        ordered = jnp.dot(tmap[t], stored, preferred_element_type=f32)
        for b in range(8):
            v = CH[t, b : b + 1] * ordered[:, :128]
            for m in range(1, MOST):
                v = v + CH[t, m * 8 + b : m * 8 + b + 1] * ordered[:, 128 * m : 128 * m + 128]
            TV[t, b] = v.astype(bf16)

    teacher(0)
    teacher(1)
    group = near.at[pl.ds(0, 15)]
    remote(group, group, xsem.at[0], xsem.at[1], plane[0]).wait()
    mid[0], mid[1] = merge([near[i] for i in range(16)])
    for device in line:
        remote(mid, far.at[x * 2 + c], xsem.at[2], xsem.at[3], device).start()
    far[x * 2 + c] = mid[...]
    teacher(2)
    teacher(3)
    group = far.at[pl.ds(0, 7)]
    remote(group, group, xsem.at[2], xsem.at[3], line[0]).wait()
    top, total = merge([far[i] for i in range(8)])

    log_norm = top[0:4] + jnp.log(total[0:4])
    tail = extra[0:4]
    weight = extra[4:8]
    kept = jnp.log(1.0 - tail) - top[4:8]
    tail_prob = tail / UNLISTED
    tail_log = jnp.log(tail_prob)

    def column(v, t):
        return jnp.broadcast_to(v[t : t + 1], (128, 128)).T

    lmsg[...] = jnp.zeros((8, 128), f32)
    for t in range(N):
        r = slice(128 * t, 128 * t + 128)
        norm_c, weight_c, kept_c = column(log_norm, t), column(weight, t), column(kept, t)
        prob_c, log_c = column(tail_prob, t), column(tail_log, t)
        acc = jnp.zeros((128, 128), f32)
        for b in range(8):
            scores = L[r, 128 * b : 128 * b + 128]
            on = CH[t, b : b + 1] + CH[t, 8 + b : 9 + b] + CH[t, 16 + b : 17 + b] + CH[t, 24 + b : 25 + b]
            off = 1.0 - on
            listed_log = TV[t, b].astype(f32) + kept_c
            q = on * jnp.exp(listed_log) + off * prob_c
            log_q = on * listed_log + off * log_c
            gap = scores - norm_c
            g = (weight_c * (jnp.exp(gap) - q)).astype(bf16)
            gl[r, 128 * b : 128 * b + 128] = g
            g = g.reshape(4, 2, 16, 128)
            far_gl[c, 4 * t : 4 * t + 4, :, 128 * b : 128 * b + 128] = g[:, 1]
            far_gl[1 - c, 4 * t : 4 * t + 4, :, 128 * b : 128 * b + 128] = g[:, 0]
            acc = acc + q * (log_q - gap)
        lmsg[t : t + 1] = jnp.sum(acc.T, axis=0, keepdims=True)

    stores = [None, None]
    count = [0]

    def head_pieces(n):
        lo = count[0]
        count[0] = lo + n

        def piece(i, carry):
            some = pl.ds(pl.multiple_of(i * PIECE, PIECE), PIECE)
            gh[some, :] = lax.dot_general(
                full[:, :, :, :, some].reshape(512, PIECE), gl[...], (((0,), (0,)), ((), ())),
                preferred_element_type=f32,
            ).astype(bf16)
            return carry

        lax.fori_loop(lo, lo + n, piece, 0)

    chunks = [
        scatter_chunk(pos, f, far_gl, w, part, cs, cr, bs, br, bsy, bry, kept_rows, ps, pr, gx, rcsem, rbsem, psend, precv)
        for f in range(NS)
    ]
    for tick in range(NS + OFF[-1]):
        for f in reversed(range(NS)):
            if tick - f in OFF:
                next(chunks[f], None)
        if tick == 0:
            for device in plane:
                remote(lmsg, lnear.at[z * N + y], xsem.at[4], xsem.at[5], device).start()
            lnear[z * N + y] = lmsg[...]
        if tick == OFF[1] + 3:
            group = lnear.at[pl.ds(0, 15)]
            remote(group, group, xsem.at[4], xsem.at[5], plane[0]).wait()
            total = lnear[0]
            for i in range(1, 16):
                total = total + lnear[i]
            lmid[...] = total
            for device in line:
                remote(lmid, lfar.at[x * 2 + c], xsem.at[6], xsem.at[7], device).start()
            lfar[x * 2 + c] = lmid[...]
        if tick in FILL:
            head_pieces(FILL[tick])
    group = lfar.at[pl.ds(0, 7)]
    remote(group, group, xsem.at[6], xsem.at[7], line[0]).wait()
    total = lfar[0]
    for i in range(1, 8):
        total = total + lfar[i]
    row = jnp.sum(jnp.where(iota((8, 128), 0) == x, total, 0.0), axis=0, keepdims=True)
    lanes = iota((128, 128), 1)
    pick = jnp.where((iota((128, 128), 0) == (z * 2 + c) * 16 + y * 4 + lanes) & (lanes < 4), 1.0, 0.0)
    loss[...] = jnp.dot(
        jnp.broadcast_to(row, (8, 128)), pick, preferred_element_type=f32, precision=lax.Precision.HIGHEST
    )


UNLISTED = 98304.0


def step(hidden, teacher, lists, reader, tail, weight, head):
    bf16, f32 = jnp.bfloat16, jnp.float32
    V = pltpu.VMEM
    return pl.pallas_call(
        step_kernel,
        out_shape=(
            jax.ShapeDtypeStruct((8, 128), f32),
            jax.ShapeDtypeStruct((4, D), bf16),
            pltpu.VMEM(head.shape, bf16),
        ),
        in_specs=[VM, VM, VM, VM, VM, VM, ANY],
        out_specs=(VM, VM, VM),
        scratch_shapes=[
            V((128, 16, 128), bf16), V((N, 128, 128), bf16), V((N, 128), f32), V((8, 128), f32), V((N, 32, 128), f32),
            V((N, N, 2, 16, D), bf16),
            V((128, 16, 128), bf16),
            V((N, 4, D), bf16),
            V((16, D), f32),
            V(head.shape, bf16),
            V((512, 1024), f32),
            V((512, 1024), bf16),
            V((2, 16, 16, 1024), bf16),
            V((2048, 128), f32),
            V((N, 8, 128, 128), bf16),
            V((2, 8, 128), f32), V((16, 2, 8, 128), f32), V((2, 8, 128), f32), V((8, 2, 8, 128), f32),
            V((8, 128), f32), V((16, 8, 128), f32), V((8, 128), f32), V((8, 8, 128), f32),
            V((NS, 16, 16, W), f32),
            V((NS, 16, 16, W), bf16), V((NS, 16, 16, W), bf16),
            V((NS, 3, N, 16, W), bf16), V((NS, 3, N, 16, W), bf16),
            V((2, N, 16, 4, WY), bf16), V((2, 3, 16, 4, WY), bf16),
            V((NS, N, 4, W), f32),
            V((NS, N, N, 4, W), bf16), V((NS, 16, 4, W), bf16),
            V((8, 128), bf16),
            DMA((NC,)),
            DMA((NC, 3)), DMA((NC, 3)),
            DMA((NC, 4)), DMA((NC, 4)),
            DMA((NC, 4, 4)), DMA((NC, 4, 4)),
            DMA((NC, 4, 4)), DMA((NC, 4, 4)),
            DMA, DMA, DMA((2,)), REGULAR, REGULAR, REGULAR,
            DMA((8,)),
            DMA((2, NS)), DMA((2, NS, 3)), DMA((NS,)), DMA((NS,)), DMA((2,)),
        ],
        compiler_params=pltpu.CompilerParams(collective_id=0, has_side_effects=True, vmem_limit_bytes=53 << 20),
        name="step",
    )(hidden, teacher, lists, reader, tail, weight, head)


def on_device(
    hidden_states, head_weight, teacher_logits, block_lists, row_reader, tail_mass, token_weight
):
    row_loss, grad_hidden, grad_head = step(
        hidden_states, teacher_logits[:, :, 0, :], block_lists, row_reader, tail_mass.reshape(N, 128), token_weight.reshape(N, 128), head_weight
    )
    token_loss = row_loss[0, :4]
    return (token_loss, grad_head, grad_hidden)


def solution(mesh):
    split = Mesh(mesh.devices.reshape(N, N, N, 2), AXES)
    return jax.shard_map(
        on_device,
        mesh=split,
        in_specs=(P(AXES, None), P(None, AXES), P(None, None, AXES, None), P(), P(), P(), P()),
        out_specs=(P(AXES), P(None, AXES), P(AXES, None)),
        check_vma=False,
    )
```
